32 devices in a mesh: ctx: 8 (over z, x), head: 4 (over y, core).
Axes of the slice: x: 2, y: 2, z: 4, core: 2. Of those that a mesh axis runs over, the one named last changes fastest.
Arguments:
- queries: bfloat16 [2048, 4096], P('ctx', 'head'), may hold values from -6 to 6
- key_rows: bfloat16 [2048, 4096], P('ctx', 'head'), may hold values from -6 to 6
- value_rows: bfloat16 [2048, 4096], P('ctx', 'head'), may hold values from -6 to 6
- norm_gain: float32 [4096], P('head'), may hold values from 0.25 to 1.75
- out_weight: bfloat16 [4096, 6144], P('head'), may hold values from -0.09375 to 0.09375
- out_cotangent: bfloat16 [2048, 6144], P(('ctx', 'head')), may hold values from -6 to 6
Outputs:
- layer_out: bfloat16 [2048, 6144], P(('ctx', 'head'))
- query_grad: bfloat16 [2048, 4096], P('ctx', 'head')
- key_grad: bfloat16 [2048, 4096], P('ctx', 'head')
- value_grad: bfloat16 [2048, 4096], P('ctx', 'head')
The draws below stay inside these ranges and needn't reach their ends.
All inputs are finite; a program needn't handle non-finite values.
Results may differ from the reference program's by a relative error of at most 0.0065.
Values may be sent and summed in bfloat16 or wider, within the bound.
No kernel may reach another device: no remote copies, remote signals or barrier semaphores. Data moves between devices by JAX's collectives and lax.ppermute only.
A program may use at most 128 MiB of HBM per device.

```python
import jax
import jax.numpy as jnp
from jax import lax

D = 6144
DH = 128
H = 32
TOK_DEV = 256
TOKENS = 2048
N_CTX = 8


def block_scale(own_key, dims, cuts, smallest, high):
    loudness = 1.0
    for position, shards_of in cuts:
        steps = jax.random.uniform(jax.random.fold_in(jax.random.fold_in(own_key, 6), position), (shards_of,), jnp.float32, smallest / len(cuts), high / len(cuts))
        loudness = loudness * jnp.repeat(jnp.exp(steps), dims[position] // shards_of).reshape((-1,) + (1,) * (len(dims) - 1 - position))
    return loudness


def bell_draw(rng, extent, width, bound, pieces=(), kind=jnp.bfloat16):
    array = width * jax.random.normal(rng, extent, jnp.float32)
    if pieces:
        array = array * block_scale(rng, extent, pieces, -0.22, 0.18)
    return jnp.clip(array, -bound, bound).astype(kind)


def setup_inputs(seed: int = 0) -> dict:
    keys = jax.random.split(jax.random.key(seed), 7)
    return {
        "queries": bell_draw(keys[0], (TOKENS, H * DH), 1.0, 6.0, ((0, 8), (1, 4))),
        "key_rows": bell_draw(keys[1], (TOKENS, H * DH), 1.0, 6.0, ((0, 8), (1, 4))),
        "value_rows": bell_draw(keys[2], (TOKENS, H * DH), 1.0, 6.0, ((0, 8), (1, 4))),
        "norm_gain": jnp.clip(1.0 + 0.15 * jax.random.normal(keys[3], (H * DH,), jnp.float32), 0.25, 1.75),
        "out_weight": bell_draw(keys[4], (H * DH, D), (H * DH) ** -0.5, 0.09375, ((0, 4),)),
        "out_cotangent": bell_draw(keys[5], (TOKENS, D), 1.0, 6.0, ((0, 32),)),
    }


def rounded(values):
    return lax.optimization_barrier(values.astype(jnp.bfloat16)).astype(jnp.float32)

def normalize(hidden, gain):
    scale = lax.rsqrt(lax.optimization_barrier(jnp.mean(hidden * hidden, axis=-1, keepdims=True)) + 1e-06)
    return hidden * scale * gain

def reference(queries, key_rows, value_rows, norm_gain, out_weight, out_cotangent):
    shape = (N_CTX, TOK_DEV, H, DH)
    query_blocks = queries.reshape(shape).astype(jnp.float32)
    key_blocks = key_rows.reshape(shape).astype(jnp.float32)
    value_blocks = value_rows.reshape(shape).astype(jnp.float32)
    causal = jnp.arange(TOK_DEV)[:, None] >= jnp.arange(TOK_DEV)[None, :]
    block_state = rounded(jnp.einsum('cthd,cthe->chde', key_blocks, value_blocks))
    zero_state = jnp.zeros_like(block_state[:1])
    prefix_state = rounded(jnp.concatenate([zero_state, jnp.cumsum(block_state, axis=0)[:-1]], axis=0))
    scores = jnp.einsum('cthd,cshd->chts', query_blocks, key_blocks)
    inner = rounded(jnp.where(causal, scores, 0.0))
    attn = jnp.einsum('chts,cshe->cthe', inner, value_blocks) + jnp.einsum('cthd,chde->cthe', query_blocks, prefix_state)
    gain = norm_gain.reshape(H, DH)
    normed = normalize(attn, gain).astype(jnp.bfloat16).reshape(TOKENS, H * DH)
    layer_out = jnp.dot(normed, out_weight, preferred_element_type=jnp.float32).astype(jnp.bfloat16)
    normed_grad = jnp.dot(out_cotangent, out_weight.T, preferred_element_type=jnp.float32).reshape(shape)
    unused, pullback = jax.vjp(lambda hidden: normalize(hidden, gain), attn)
    attn_grad = rounded(pullback(normed_grad)[0])
    grad_state = rounded(jnp.einsum('cthd,cthe->chde', query_blocks, attn_grad))
    flipped = jnp.cumsum(grad_state[::-1], axis=0)[::-1]
    suffix_state = rounded(jnp.concatenate([flipped[1:], zero_state], axis=0))
    inner_grad = rounded(jnp.where(causal, jnp.einsum('cthe,cshe->chts', attn_grad, value_blocks), 0.0))
    query_grad = jnp.einsum('chts,cshd->cthd', inner_grad, key_blocks) + jnp.einsum('cthe,chde->cthd', attn_grad, prefix_state)
    key_grad = jnp.einsum('chts,cthd->cshd', inner_grad, query_blocks) + jnp.einsum('cthe,chde->cthd', value_blocks, suffix_state)
    value_grad = jnp.einsum('chts,cthe->cshe', inner, attn_grad) + jnp.einsum('cthd,chde->cthe', key_blocks, suffix_state)
    flat = (TOKENS, H * DH)
    return (layer_out, query_grad.reshape(flat).astype(jnp.bfloat16), key_grad.reshape(flat).astype(jnp.bfloat16), value_grad.reshape(flat).astype(jnp.bfloat16))
```

```python
import functools

import jax
import jax.numpy as jnp
from jax import lax
from jax.experimental import pallas as pl
from jax.experimental.pallas import tpu as pltpu
from jax.sharding import PartitionSpec as P

DH = 128
EPS = 1e-06
CHUNKS = 3
F32 = jnp.float32
BF16 = jnp.bfloat16


def dot(a, b, ca, cb):
    return lax.dot_general(a, b, (((ca,), (cb,)), ((), ())), preferred_element_type=F32)


def call(kernel, name, outs, args, flops, limit=8):
    moved = sum(a.size * a.dtype.itemsize for a in args) + sum(
        o.size * o.dtype.itemsize for o in outs
    )
    return pl.pallas_call(
        kernel,
        name=name,
        out_shape=outs,
        in_specs=[pl.BlockSpec(memory_space=pltpu.VMEM)] * len(args),
        out_specs=[pl.BlockSpec(memory_space=pltpu.VMEM)] * len(outs),
        compiler_params=pltpu.CompilerParams(vmem_limit_bytes=limit << 20),
        cost_estimate=pl.CostEstimate(flops=flops, bytes_accessed=moved, transcendentals=0),
    )(*args)


def shaped(shape, dtype):
    return jax.ShapeDtypeStruct(shape, dtype)


def lanes(head):
    return pl.ds(pl.multiple_of(head * DH, DH), DH)


def side():
    return lax.rem(lax.axis_index("ctx"), 2)


def place(k, n):
    out = 0
    bit = 1
    while bit < n:
        out = out * 2 + (k // bit) % 2
        bit *= 2
    return out


def state_kernel(half, key_ref, value_ref, keep_ref, send_ref):
    x = side()
    for mine, ref in ((1 - x, send_ref), (x, keep_ref)):
        for i in range(half):
            cols = lanes(mine * half + i)
            ref[i] = dot(key_ref[:, cols], value_ref[:, cols], 0, 0).astype(BF16)


def causal_mask(n):
    row = lax.broadcasted_iota(jnp.int32, (n, n), 0)
    col = lax.broadcasted_iota(jnp.int32, (n, n), 1)
    return col <= row


def inner_kernel(heads, query_ref, key_ref, value_ref, inner_ref, intra_ref):
    mask = causal_mask(query_ref.shape[0])
    for h in range(heads):
        cols = slice(h * DH, (h + 1) * DH)
        scores = dot(query_ref[:, cols], key_ref[:, cols], 1, 1)
        inner = jnp.where(mask, scores, 0.0).astype(BF16)
        inner_ref[h] = inner
        intra_ref[:, cols] = dot(inner, value_ref[:, cols], 1, 0)


def norm_kernel(half, n_head, query_ref, intra_ref, own_ref, other_ref, gain_ref, attn_ref, normed_ref):
    x = side()
    me = lax.axis_index("head")
    rows = query_ref.shape[0] // n_head
    for mine, ref in ((x, own_ref), (1 - x, other_ref)):
        for i in range(half):
            cols = lanes(mine * half + i)
            attn = intra_ref[:, cols] + dot(query_ref[:, cols], ref[i], 1, 0)
            attn_ref[:, cols] = attn
            scale = lax.rsqrt(jnp.mean(attn * attn, axis=-1, keepdims=True) + EPS)
            normed = (attn * scale * gain_ref[:, cols]).astype(BF16)
            for j in range(n_head):
                start = pl.multiple_of(place(lax.bitwise_xor(me, j), n_head) * rows, rows)
                normed_ref[pl.ds(start, rows), cols] = normed[j * rows : (j + 1) * rows]


def grad_kernel(half, n_head, query_ref, attn_ref, back_ref, gain_ref, grad_ref, keep_ref, send_ref):
    x = side()
    me = lax.axis_index("head")
    rows = query_ref.shape[0] // n_head
    for mine, ref in ((1 - x, send_ref), (x, keep_ref)):
        for i in range(half):
            cols = lanes(mine * half + i)
            attn = attn_ref[:, cols]
            parts = []
            for j in range(n_head):
                start = pl.multiple_of(place(lax.bitwise_xor(me, j), n_head) * rows, rows)
                parts.append(back_ref[pl.ds(start, rows), cols])
            back = jnp.concatenate(parts, axis=0) * gain_ref[:, cols]
            scale = lax.rsqrt(jnp.mean(attn * attn, axis=-1, keepdims=True) + EPS)
            lean = jnp.mean(back * attn, axis=-1, keepdims=True)
            grad = (scale * (back - attn * (scale * scale * lean))).astype(BF16)
            grad_ref[:, cols] = grad
            ref[i] = dot(query_ref[:, cols], grad, 0, 0).astype(BF16)


def local_grad_kernel(
    half, query_ref, key_ref, value_ref, inner_ref, grad_ref, own_ref, other_ref,
    query_grad_ref, key_part_ref, value_part_ref,
):
    x = side()
    mask = causal_mask(query_ref.shape[0])
    for mine, ref in ((x, own_ref), (1 - x, other_ref)):
        for i in range(half):
            h = mine * half + i
            cols = lanes(h)
            grad = grad_ref[:, cols]
            inner_grad = jnp.where(mask, dot(grad, value_ref[:, cols], 1, 1), 0.0).astype(BF16)
            query_grad_ref[:, cols] = (
                dot(inner_grad, key_ref[:, cols], 1, 0) + dot(grad, ref[i], 1, 1)
            ).astype(BF16)
            key_part_ref[:, cols] = dot(inner_grad, query_ref[:, cols], 0, 0)
            value_part_ref[:, cols] = dot(inner_ref[h], grad, 0, 0)


def final_grad_kernel(
    half, key_ref, value_ref, key_part_ref, value_part_ref, own_ref, other_ref, key_grad_ref, value_grad_ref
):
    x = side()
    for mine, ref in ((x, own_ref), (1 - x, other_ref)):
        for i in range(half):
            cols = lanes(mine * half + i)
            state = ref[i]
            key_grad_ref[:, cols] = (
                key_part_ref[:, cols] + dot(value_ref[:, cols], state, 1, 1)
            ).astype(BF16)
            value_grad_ref[:, cols] = (
                value_part_ref[:, cols] + dot(key_ref[:, cols], state, 1, 0)
            ).astype(BF16)


def back_kernel(n_head, *refs):
    piece_refs, (weight_ref, out_ref, full_ref) = refs[:n_head], refs[n_head:]
    rows = piece_refs[0].shape[0]

    @pl.when(pl.program_id(0) == 0)
    def _():
        for j in range(n_head):
            full_ref[j * rows : (j + 1) * rows] = piece_refs[j][...]

    out_ref[...] = dot(full_ref[...], weight_ref[...], 1, 1)


def back_matmul(pieces, weight):
    n = len(pieces)
    rows, depth = pieces[0].shape
    features = weight.shape[0]
    step = 256
    whole = pl.BlockSpec((rows, depth), lambda i: (0, 0))
    return pl.pallas_call(
        functools.partial(back_kernel, n),
        name="back_matmul",
        grid=(features // step,),
        out_shape=shaped((n * rows, features), F32),
        in_specs=[whole] * n + [pl.BlockSpec((step, depth), lambda i: (i, 0))],
        out_specs=pl.BlockSpec((n * rows, step), lambda i: (0, i)),
        scratch_shapes=[pltpu.VMEM((n * rows, depth), BF16)],
        compiler_params=pltpu.CompilerParams(vmem_limit_bytes=24 << 20),
        cost_estimate=pl.CostEstimate(
            flops=2 * n * rows * depth * features,
            bytes_accessed=2 * features * depth + 2 * n * rows * depth + 4 * n * rows * features,
            transcendentals=0,
        ),
    )(*pieces, weight)


def forward_kernel(normed_ref, weight_ref, keep_ref, send_ref):
    half = keep_ref.shape[0]
    out = dot(normed_ref[...], weight_ref[...], 1, 0)
    keep_ref[...] = out[:half]
    send_ref[...] = out[half:].astype(BF16)


def forward_matmul(normed, weight, chunk, width):
    tokens, features = normed.shape
    step = 512
    first = chunk * width // step
    half = tokens // 2
    return pl.pallas_call(
        forward_kernel,
        name="forward_matmul",
        grid=(width // step,),
        out_shape=[shaped((half, width), F32), shaped((half, width), BF16)],
        in_specs=[
            pl.BlockSpec((tokens, features), lambda i: (0, 0)),
            pl.BlockSpec((features, step), lambda i: (0, first + i)),
        ],
        out_specs=[pl.BlockSpec((half, step), lambda i: (0, i))] * 2,
        compiler_params=pltpu.CompilerParams(vmem_limit_bytes=16 << 20),
        cost_estimate=pl.CostEstimate(
            flops=2 * tokens * features * width,
            bytes_accessed=2 * features * width + 2 * tokens * features + 6 * half * width,
            transcendentals=0,
        ),
    )(normed, weight)


def swap(value, axis, size, bit):
    return lax.ppermute(value, axis, [(i, i ^ bit) for i in range(size)])


def exclusive_scan(keep, send, n_ctx, forward):
    position = lax.axis_index("ctx")

    def later(bit):
        on = (position // bit) % 2 == 1
        return on if forward else jnp.logical_not(on)

    received = swap(send, "ctx", n_ctx, 1)
    total = keep.astype(F32) + received.astype(F32)
    before = jnp.zeros_like(total)
    bit = 2
    while bit < n_ctx:
        partner = swap(total.astype(BF16), "ctx", n_ctx, bit).astype(F32)
        before = before + jnp.where(later(bit), partner, 0.0)
        total = total + partner
        bit *= 2
    last = later(1)
    own = before + jnp.where(last, received.astype(F32), 0.0)
    partner = before + jnp.where(last, 0.0, keep.astype(F32))
    other = swap(partner.astype(BF16), "ctx", n_ctx, 1)
    return own.astype(BF16), other


def per_device(n_ctx, n_head, queries, key_rows, value_rows, norm_gain, out_weight, out_cotangent):
    tokens, width = queries.shape
    heads = width // DH
    half = heads // 2
    model = out_weight.shape[1]
    gain = norm_gain.reshape(1, width)
    part = [shaped((half, DH, DH), BF16)] * 2
    unit = 2 * tokens * DH * DH * heads

    pieces = [out_cotangent]
    bit = 1
    far = swap(out_cotangent, "head", n_head, n_head // 2)
    near = [out_cotangent]
    far = [far]
    while bit < n_head // 2:
        near = near + [swap(p, "head", n_head, bit) for p in near]
        far = far + [swap(p, "head", n_head, bit) for p in far]
        bit *= 2
    pieces = near + far

    keep, send = call(
        functools.partial(state_kernel, half), "state", part, (key_rows, value_rows), unit
    )
    own, other = exclusive_scan(keep, send, n_ctx, True)
    inner, intra = call(
        functools.partial(inner_kernel, heads),
        "inner",
        [shaped((heads, tokens, tokens), BF16), shaped((tokens, width), F32)],
        (queries, key_rows, value_rows),
        4 * unit,
    )
    order = [place(k, n_head) for k in range(n_head)]
    ordered = [None] * n_head
    for k, piece in enumerate(pieces):
        ordered[order[k]] = piece
    back = back_matmul(ordered, out_weight)

    attn, normed = call(
        functools.partial(norm_kernel, half, n_head),
        "norm",
        [shaped((tokens, width), F32), shaped((tokens, width), BF16)],
        (queries, intra, own, other, gain),
        unit,
    )
    grad, keep, send = call(
        functools.partial(grad_kernel, half, n_head),
        "grad",
        [shaped((tokens, width), BF16)] + part,
        (queries, attn, back, gain),
        unit,
    )
    later_own, later_other = exclusive_scan(keep, send, n_ctx, False)

    outs = []
    span = model // CHUNKS
    for chunk in range(CHUNKS):
        kept, sent = forward_matmul(normed, out_weight, chunk, span)
        bit = 1
        while True:
            kept = kept + swap(sent, "head", n_head, bit).astype(F32)
            bit *= 2
            if bit == n_head:
                break
            rows = kept.shape[0] // 2
            kept, sent = kept[:rows], kept[rows:].astype(BF16)
        outs.append(kept.astype(BF16))
    layer_out = jnp.concatenate(outs, axis=1)

    query_grad, key_part, value_part = call(
        functools.partial(local_grad_kernel, half),
        "local_grad",
        [shaped((tokens, width), BF16), shaped((tokens, width), F32), shaped((tokens, width), F32)],
        (queries, key_rows, value_rows, inner, grad, own, other),
        8 * unit,
    )
    key_grad, value_grad = call(
        functools.partial(final_grad_kernel, half),
        "final_grad",
        [shaped((tokens, width), BF16)] * 2,
        (key_rows, value_rows, key_part, value_part, later_own, later_other),
        2 * unit,
    )
    return layer_out, query_grad, key_grad, value_grad


def solution(mesh):
    in_specs = (
        P("ctx", "head"),
        P("ctx", "head"),
        P("ctx", "head"),
        P("head"),
        P("head", None),
        P(("ctx", "head"), None),
    )
    out_specs = (P(("ctx", "head"), None), P("ctx", "head"), P("ctx", "head"), P("ctx", "head"))
    body = functools.partial(per_device, mesh.shape["ctx"], mesh.shape["head"])
    return jax.shard_map(body, mesh=mesh, in_specs=in_specs, out_specs=out_specs, check_vma=False)
```

```python
import functools

import jax
import jax.numpy as jnp
from jax import lax
from jax.experimental import pallas as pl
from jax.experimental.pallas import tpu as pltpu
from jax.sharding import PartitionSpec as P


DH = 128
EPS = 1e-06
GROUP = 4
BACK_CHUNKS = 2
PARTS = 3
FORWARD = (((0, 0, 3), (1, 0, 1)), ((1, 1, 3),))
LOADS = 4
F32 = jnp.float32
BF16 = jnp.bfloat16


def dot(a, b, ca, cb):
    return lax.dot_general(a, b, (((ca,), (cb,)), ((), ())), preferred_element_type=F32)


def call(kernel, outs, args, flops, limit=8):
    moved = sum(a.size * a.dtype.itemsize for a in args) + sum(
        o.size * o.dtype.itemsize for o in outs
    )
    return pl.pallas_call(
        kernel,
        out_shape=outs,
        in_specs=[pl.BlockSpec(memory_space=pltpu.VMEM)] * len(args),
        out_specs=[pl.BlockSpec(memory_space=pltpu.VMEM)] * len(outs),
        compiler_params=pltpu.CompilerParams(vmem_limit_bytes=limit << 20),
        cost_estimate=pl.CostEstimate(flops=flops, bytes_accessed=moved, transcendentals=0),
    )(*args)


def shaped(shape, dtype):
    return jax.ShapeDtypeStruct(shape, dtype)


def in_hbm(value):
    return pltpu.with_memory_space_constraint(value, pltpu.HBM)


def lanes(head):
    return pl.ds(pl.multiple_of(head * DH, DH), DH)


def member(group, k):
    return lax.bitwise_xor(lax.rem(lax.axis_index("ctx"), group), k)


def place(k, n):
    out = 0
    bit = 1
    while bit < n:
        out = out * 2 + (k // bit) % 2
        bit *= 2
    return out


def start_all(copies):
    for copy in copies:
        copy.start()
    return copies


def wait_all(copies):
    for copy in copies:
        copy.wait()


def columns(group, k, width):
    return pl.ds(pl.multiple_of(member(group, k) * width, width), width)


def state_kernel(group, share, ks, first, chunks, *refs):
    key_hbm, value_hbm, query_hbm, cotangent_hbm, *refs = refs
    state_refs, (key_ref, value_ref, *refs, sems) = refs[: len(ks)], refs[len(ks) :]
    width = share * DH
    depth = cotangent_hbm.shape[1] // chunks
    query_refs = refs[: 2 if 0 in ks else 0]
    part_refs = refs[len(query_refs) :]
    pairs = []
    for n, k in enumerate(ks):
        cols, here = columns(group, k, width), pl.ds(n * width, width)
        pairs.append((key_hbm.at[:, cols], key_ref.at[:, here]))
        pairs.append((value_hbm.at[:, cols], value_ref.at[:, here]))
    for n, ref in enumerate(part_refs):
        pairs.append((cotangent_hbm.at[:, pl.ds((first + n) * depth, depth)], ref))
    if query_refs:
        for k in range(group):
            ref = query_refs[min(k, 1)].at[:, pl.ds(max(k - 1, 0) * width, width)]
            pairs.append((query_hbm.at[:, columns(group, k, width)], ref))
    copies = start_all(
        [pltpu.make_async_copy(src, dst, sems.at[n]) for n, (src, dst) in enumerate(pairs)]
    )
    for n in range(len(ks)):
        wait_all(copies[2 * n : 2 * n + 2])
        for i in range(share):
            h = slice((n * share + i) * DH, (n * share + i + 1) * DH)
            state_refs[n][i] = dot(key_ref[:, h], value_ref[:, h], 0, 0).astype(BF16)
    wait_all(copies[2 * len(ks) :])


def block_states(group, share, ks, args, first, count, chunks):
    tokens = args[0].shape[0]
    rows, model = args[3].shape
    width = share * DH
    outs = [shaped((share, DH, DH), BF16)] * len(ks) + [shaped((tokens, len(ks) * width), BF16)] * 2
    if 0 in ks:
        outs += [shaped((tokens, width), BF16), shaped((tokens, (group - 1) * width), BF16)]
    outs += [shaped((rows, model // chunks), BF16)] * count
    return pl.pallas_call(
        functools.partial(state_kernel, group, share, ks, first, chunks),
        name="state",
        out_shape=outs,
        in_specs=[pl.BlockSpec(memory_space=pltpu.HBM)] * 4,
        out_specs=[pl.BlockSpec(memory_space=pltpu.VMEM)] * len(outs),
        scratch_shapes=[pltpu.SemaphoreType.DMA((2 * len(ks) + group + count,))],
        compiler_params=pltpu.CompilerParams(vmem_limit_bytes=4 << 20),
        cost_estimate=pl.CostEstimate(
            flops=2 * tokens * DH * width * len(ks), bytes_accessed=1 << 20, transcendentals=0
        ),
    )(*map(in_hbm, args))


def causal_mask(n):
    row = lax.broadcasted_iota(jnp.int32, (n, n), 0)
    col = lax.broadcasted_iota(jnp.int32, (n, n), 1)
    return col <= row


def load_copies(chunk, weight_hbm, weight_ref, sems):
    rows = weight_ref.shape[0] // LOADS
    width = weight_ref.shape[1]
    return [
        pltpu.make_async_copy(
            weight_hbm.at[pl.ds(n * rows, rows), pl.ds(chunk * width, width)],
            weight_ref.at[pl.ds(n * rows, rows)],
            sems.at[n],
        )
        for n in range(LOADS)
    ]


def loading_call(kernel, outs, args, weight, chunk, chunks, flops):
    features, model = weight.shape
    moved = 2 * features * model // chunks
    vmem = pl.BlockSpec(memory_space=pltpu.VMEM)
    *outs, weight = pl.pallas_call(
        functools.partial(kernel, chunk),
        out_shape=outs + [pltpu.VMEM((features, model // chunks), BF16)],
        in_specs=[vmem] * len(args) + [pl.BlockSpec(memory_space=pltpu.HBM)],
        out_specs=[vmem] * (len(outs) + 1),
        scratch_shapes=[pltpu.SemaphoreType.DMA((LOADS,))],
        compiler_params=pltpu.CompilerParams(vmem_limit_bytes=8 << 20),
        cost_estimate=pl.CostEstimate(flops=flops, bytes_accessed=moved, transcendentals=0),
    )(*args, in_hbm(weight))
    return outs, weight


def load_kernel(chunk, weight_hbm, weight_ref, sems):
    wait_all(start_all(load_copies(chunk, weight_hbm, weight_ref, sems)))


def inner_kernel(*refs):
    queries, keys, values, inners, intras = (refs[n : n + 2] for n in range(0, 10, 2))
    mask = causal_mask(queries[0].shape[0])
    for n in range(2):
        for i in range(inners[n].shape[0]):
            h = slice(i * DH, (i + 1) * DH)
            scores = dot(queries[n][:, h], keys[n][:, h], 1, 1)
            inner = jnp.where(mask, scores, 0.0).astype(BF16)
            inners[n][i] = inner
            intras[n][:, h] = dot(inner, values[n][:, h], 1, 0)


def member_heads(group, share, ks):
    for n, k in enumerate(ks):
        for i in range(share):
            here = slice((n * share + i) * DH, (n * share + i + 1) * DH)
            yield here, lanes(member(group, k) * share + i), n, i


def row_starts(n_head, rows):
    me = lax.axis_index("head")
    return [
        pl.multiple_of(place(lax.bitwise_xor(me, j), n_head) * rows, rows) for j in range(n_head)
    ]


def norm_kernel(group, share, ks, n_head, query_ref, intra_ref, gain_ref, *refs):
    state_refs, (attn_ref, normed_ref) = refs[: len(ks)], refs[len(ks) :]
    rows = query_ref.shape[0] // n_head
    starts = row_starts(n_head, rows)
    for h, cols, n, i in member_heads(group, share, ks):
        attn = intra_ref[:, h] + dot(query_ref[:, h], state_refs[n][i], 1, 0)
        attn_ref[:, h] = attn
        scale = lax.rsqrt(jnp.mean(attn * attn, axis=-1, keepdims=True) + EPS)
        normed = (attn * scale * gain_ref[:, cols]).astype(BF16)
        for j, start in enumerate(starts):
            normed_ref[pl.ds(start, rows), h] = normed[j * rows : (j + 1) * rows]


def grad_kernel(group, share, ks, n_head, query_ref, attn_ref, back_ref, gain_ref, grad_ref, *state_refs):
    rows = query_ref.shape[0] // n_head
    starts = row_starts(n_head, rows)
    for h, cols, n, i in member_heads(group, share, ks):
        attn = attn_ref[:, h]
        back = jnp.concatenate([back_ref[pl.ds(start, rows), cols] for start in starts], axis=0)
        back = back * gain_ref[:, cols]
        scale = lax.rsqrt(jnp.mean(attn * attn, axis=-1, keepdims=True) + EPS)
        lean = jnp.mean(back * attn, axis=-1, keepdims=True)
        grad = (scale * (back - attn * (scale * scale * lean))).astype(BF16)
        grad_ref[:, h] = grad
        state_refs[n][i] = dot(query_ref[:, h], grad, 0, 0).astype(BF16)


def local_grad_kernel(group, share, sides, *refs):
    state_refs, refs = refs[:group], refs[group:]
    mask = causal_mask(refs[0].shape[0])
    query_grad_ref = refs[10]
    for side, ks in enumerate(sides):
        query_ref, key_ref, value_ref, inner_ref, grad_ref = refs[side:10:2]
        key_part_ref, value_part_ref = refs[11 + side], refs[13 + side]
        for h, cols, n, i in member_heads(group, share, ks):
            grad = grad_ref[:, h]
            inner_grad = jnp.where(mask, dot(grad, value_ref[:, h], 1, 1), 0.0).astype(BF16)
            query_grad_ref[:, cols] = (
                dot(inner_grad, key_ref[:, h], 1, 0) + dot(grad, state_refs[ks[n]][i], 1, 1)
            ).astype(BF16)
            key_part_ref[:, h] = dot(inner_grad, query_ref[:, h], 0, 0)
            value_part_ref[:, h] = dot(inner_ref[n * share + i], grad, 0, 0)


def final_kernel(group, share, ks, starts, key_ref, value_ref, key_part_ref, value_part_ref, *refs):
    *refs, key_grad_hbm, value_grad_hbm, out_hbm, key_grad_ref, value_grad_ref, out_ref, sems, out_sems = refs
    state_refs, refs = refs[: len(ks)], refs[len(ks) :]
    copies = []
    for n, first in enumerate(starts):
        keep_ref, received_ref = refs[2 * n], refs[2 * n + 1]
        span = keep_ref.shape[1]
        here = pl.ds(first - starts[0], span)
        out_ref[:, here] = (keep_ref[...] + received_ref[...].astype(F32)).astype(BF16)
        target = out_hbm.at[:, pl.ds(first, span)]
        copies += start_all([pltpu.make_async_copy(out_ref.at[:, here], target, out_sems.at[n])])
    for h, cols, n, i in member_heads(group, share, ks):
        state = state_refs[n][i]
        key_grad = key_part_ref[:, h] + dot(value_ref[:, h], state, 1, 1)
        key_grad_ref[:, h] = key_grad.astype(BF16)
        value_grad = value_part_ref[:, h] + dot(key_ref[:, h], state, 1, 0)
        value_grad_ref[:, h] = value_grad.astype(BF16)
        at = n * share + i
        copies += start_all(
            [
                pltpu.make_async_copy(key_grad_ref.at[:, h], key_grad_hbm.at[:, cols], sems.at[0, at]),
                pltpu.make_async_copy(value_grad_ref.at[:, h], value_grad_hbm.at[:, cols], sems.at[1, at]),
            ]
        )
    wait_all(copies)


def final_part(group, share, ks, args, chunks, model, before):
    tokens, width = args[0].shape
    starts = [first for first, _, _ in chunks]
    args = args + [ref for _, *pair in chunks for ref in pair]
    rows = chunks[0][1].shape[0]
    span = sum(kept.shape[1] for _, kept, _ in chunks)
    buffer = pltpu.VMEM((tokens, width), BF16)
    out = shaped((tokens, group * share * DH), BF16)
    return pl.pallas_call(
        functools.partial(final_kernel, group, share, ks, starts),
        name="final",
        out_shape=[out, out, shaped((rows, model), BF16)],
        in_specs=[pl.BlockSpec(memory_space=pltpu.VMEM)] * len(args)
        + [pl.BlockSpec(memory_space=pltpu.HBM)] * len(before),
        out_specs=[pl.BlockSpec(memory_space=pltpu.HBM)] * 3,
        input_output_aliases={len(args) + n: n for n in range(len(before))},
        scratch_shapes=[
            buffer,
            buffer,
            pltpu.VMEM((rows, span), BF16),
            pltpu.SemaphoreType.DMA((2, len(ks) * share)),
            pltpu.SemaphoreType.DMA((len(chunks),)),
        ],
        compiler_params=pltpu.CompilerParams(vmem_limit_bytes=4 << 20),
        cost_estimate=pl.CostEstimate(
            flops=4 * tokens * DH * width, bytes_accessed=3 << 20, transcendentals=0
        ),
    )(*args, *before)


def back_kernel(n_head, load, chunk, *refs):
    piece_refs, (weight_ref, *refs) = refs[:n_head], refs[n_head:]
    if load is not None:
        before_refs, (weight_hbm, out_ref, next_ref, sems) = refs[:-4], refs[-4:]
        copies = start_all(load_copies(load, weight_hbm, next_ref, sems))
    else:
        before_refs, out_ref, copies = refs[:-1], refs[-1], []
    depth = weight_ref.shape[1]
    pieces = []
    for ref in piece_refs:
        start = chunk * depth if ref.shape[1] > depth else 0
        pieces.append(ref[:, start : start + depth])
    full = jnp.concatenate(pieces, axis=0)
    step = 256
    for i in range(weight_ref.shape[0] // step):
        cols = slice(i * step, (i + 1) * step)
        out = dot(full, weight_ref[cols], 1, 1)
        for ref in before_refs:
            out = out + ref[:, cols]
        out_ref[:, cols] = out
    wait_all(copies)


def first_back_kernel(n_head, load, *refs):
    back_kernel(n_head, load, load - 1, *refs)


def forward_kernel(group, segments, own_ref, other_ref, *refs):
    *weight_refs, keep_ref, send_ref = refs
    half = keep_ref.shape[0]
    depth = own_ref.shape[1]
    step = 512
    at = 0
    for weight_ref, (start, stop) in zip(weight_refs, segments):
        for first in range(start, stop, step):
            cols, source = slice(at, at + step), slice(first, first + step)
            out = dot(own_ref[...], weight_ref[columns(group, 0, depth), source], 1, 0)
            for k in range(1, group):
                here = slice((k - 1) * depth, k * depth)
                out = out + dot(other_ref[:, here], weight_ref[columns(group, k, depth), source], 1, 0)
            keep_ref[:, cols] = out[:half]
            send_ref[:, cols] = out[half:].astype(BF16)
            at += step


def swap(value, axis, size, bit):
    return lax.ppermute(value, axis, [(i, i ^ bit) for i in range(size)])


def total_kernel(*refs):
    total = refs[0][...].astype(F32)
    for ref in refs[1:-1]:
        total = total + ref[...].astype(F32)
    refs[-1][...] = total.astype(BF16)


def split_kernel(group, forward, *refs):
    received, partners, outs = refs[:group], refs[group:-group], refs[-group:]
    position = lax.axis_index("ctx")
    before = jnp.zeros(outs[0].shape, F32)
    for n, ref in enumerate(partners):
        high = lax.rem(lax.div(position, group << n), 2)
        before = before + (high if forward else 1 - high).astype(F32) * ref[...].astype(F32)
    terms = [ref[...].astype(F32) for ref in received]
    for k, out in enumerate(outs):
        total = before
        for j, term in enumerate(terms):
            if j != k:
                mine, its = member(group, k), member(group, j)
                counts = its < mine if forward else its > mine
                total = total + jnp.where(counts, 1.0, 0.0) * term
        out[...] = total.astype(BF16)


def exclusive_scan(states, group, n_ctx, forward):
    like = shaped(states[0].shape, BF16)
    received = [states[0]]
    received += [swap(states[k], "ctx", n_ctx, k) for k in range(1, group)]
    bit = group
    while bit < n_ctx:
        (total,) = call(total_kernel, [like], received, 0, 4)
        received.append(swap(total, "ctx", n_ctx, bit))
        bit *= 2
    own, *others = call(functools.partial(split_kernel, group, forward), [like] * group, received, 0, 4)
    return [own] + [swap(o, "ctx", n_ctx, k + 1) for k, o in enumerate(others)]


def fold_kernel(keep_ref, received_ref, kept_ref, send_ref):
    rows = kept_ref.shape[0]
    kept_ref[...] = keep_ref[:rows] + received_ref[:rows].astype(F32)
    send_ref[...] = (keep_ref[rows:] + received_ref[rows:].astype(F32)).astype(BF16)


def spread(parts, below, size):
    bit = 1
    while bit < below:
        parts = parts + [swap(p, "head", size, bit) for p in parts]
        bit *= 2
    return parts


def per_device(n_ctx, n_head, queries, key_rows, value_rows, norm_gain, out_weight, out_cotangent):
    return layer(
        n_ctx, n_head, queries, key_rows, value_rows, norm_gain, out_weight, out_cotangent
    )


def layer(n_ctx, n_head, queries, key_rows, value_rows, norm_gain, out_weight, out_cotangent):
    tokens, width = queries.shape
    heads = width // DH
    group = min(GROUP, n_ctx)
    share = heads // group
    model = out_weight.shape[1]
    gain = norm_gain.reshape(1, width)
    part = shaped((share, DH, DH), BF16)
    sides = ((0,), tuple(range(1, group)))
    sizes = [share * DH * len(ks) for ks in sides]
    unit = 2 * tokens * DH * width
    order = [place(k, n_head) for k in range(n_head)]

    args = (key_rows, value_rows, queries, out_cotangent)
    *sent, key_other, value_other, first = block_states(
        group, share, sides[1], args, 0, 1, BACK_CHUNKS
    )
    kept, key_own, value_own, *query_sides, second = block_states(
        group, share, sides[0], args, 1, 1, BACK_CHUNKS
    )
    keys, values = (key_own, key_other), (value_own, value_other)
    far = [swap(p, "head", n_head, n_head // 2) for p in (first, second)]
    near = spread([out_cotangent], n_head // 2, n_head)
    states = exclusive_scan([kept] + sent, group, n_ctx, True)
    squares = [shaped((share * len(ks), tokens, tokens), BF16) for ks in sides]
    blocks_f32 = [shaped((tokens, size), F32) for size in sizes]
    blocks_bf16 = [shaped((tokens, size), BF16) for size in sizes]
    args = [*query_sides, *keys, *values]
    outs = call(inner_kernel, squares + blocks_f32, args, 4 * unit)
    inners, intras = outs[:2], outs[2:]
    _, first_weight = loading_call(load_kernel, [], [], out_weight, 0, BACK_CHUNKS, 0)

    pieces = []
    for j in range(BACK_CHUNKS):
        ordered = [None] * n_head
        for k, piece in enumerate(near + spread([far[j]], n_head // 2, n_head)):
            ordered[order[k]] = piece
        pieces.append(ordered)
    back_shape = [shaped((tokens, width), F32)]
    flops = 2 * tokens * width * model // BACK_CHUNKS
    kernel = functools.partial(first_back_kernel, n_head)
    (back,), second_weight = loading_call(
        kernel, back_shape, pieces[0] + [first_weight], out_weight, 1, BACK_CHUNKS, flops
    )
    weights = (first_weight, second_weight)
    kernel = functools.partial(back_kernel, n_head, None, 1)
    (back,) = call(kernel, back_shape, pieces[1] + [second_weight, back], flops)

    attns, normeds = [], []
    for n, ks in enumerate(sides):
        attn, normed = call(
            functools.partial(norm_kernel, group, share, ks, n_head),
            [blocks_f32[n], blocks_bf16[n]],
            [query_sides[n], intras[n], gain] + [states[k] for k in ks],
            unit // 2,
        )
        attns.append(attn)
        normeds.append(normed)
    grads, grad_states = [], []
    for n, ks in enumerate(sides):
        grad, *state = call(
            functools.partial(grad_kernel, group, share, ks, n_head),
            [blocks_bf16[n]] + [part] * len(ks),
            [query_sides[n], attns[n], back, gain],
            unit // 2,
        )
        grads.append(grad)
        grad_states += state
    later_states = exclusive_scan(grad_states, group, n_ctx, False)

    chunks = []
    base = model // (BACK_CHUNKS * PARTS)
    done = 0
    for pieces in FORWARD:
        segments = [(start * base, stop * base) for _, start, stop in pieces]
        span = sum(stop - start for start, stop in segments)
        kept, sent = call(
            functools.partial(forward_kernel, group, segments),
            [shaped((tokens // 2, span), F32), shaped((tokens // 2, span), BF16)],
            normeds + [weights[source] for source, _, _ in pieces],
            2 * tokens * width * span,
        )
        arrived = swap(sent, "head", n_head, 1)
        bit = 2
        while bit < n_head:
            rows = kept.shape[0] // 2
            kept, sent = call(
                fold_kernel, [shaped((rows, span), F32), shaped((rows, span), BF16)], [kept, arrived], 0, 4
            )
            arrived = swap(sent, "head", n_head, bit)
            bit *= 2
        chunks.append((done, kept, arrived))
        done += span

    query_grad, *parts = call(
        functools.partial(local_grad_kernel, group, share, sides),
        [shaped((tokens, width), BF16)] + blocks_f32 * 2,
        [*states, *query_sides, *keys, *values, *inners, *grads],
        8 * unit,
    )
    finals = []
    for n, ks in enumerate(sides):
        ready = chunks[-1:] if n else chunks[:-1]
        args = [keys[n], values[n], parts[n], parts[2 + n]] + [later_states[k] for k in ks]
        finals = final_part(group, share, ks, args, ready, model, finals)
    key_grad, value_grad, layer_out = finals
    return layer_out, query_grad, key_grad, value_grad


def solution(mesh):
    in_specs = (
        P("ctx", "head"),
        P("ctx", "head"),
        P("ctx", "head"),
        P("head"),
        P("head", None),
        P(("ctx", "head"), None),
    )
    out_specs = (P(("ctx", "head"), None), P("ctx", "head"), P("ctx", "head"), P("ctx", "head"))
    body = functools.partial(per_device, mesh.shape["ctx"], mesh.shape["head"])
    return jax.shard_map(body, mesh=mesh, in_specs=in_specs, out_specs=out_specs, check_vma=False)
```

```python
import functools

import jax
import jax.numpy as jnp
from jax import lax
from jax.experimental import pallas as pl
from jax.experimental.pallas import tpu as pltpu
from jax.sharding import PartitionSpec as P


DH = 128
EPS = 1e-06
GROUP = 4
EARLY = 2
BACK_CHUNKS = 2
LOADS = 4
F32 = jnp.float32
BF16 = jnp.bfloat16


def dot(a, b, ca, cb):
    return lax.dot_general(a, b, (((ca,), (cb,)), ((), ())), preferred_element_type=F32)


def call(kernel, outs, args, flops, limit=8):
    moved = sum(a.size * a.dtype.itemsize for a in args) + sum(
        o.size * o.dtype.itemsize for o in outs
    )
    return pl.pallas_call(
        kernel,
        out_shape=outs,
        in_specs=[pl.BlockSpec(memory_space=pltpu.VMEM)] * len(args),
        out_specs=[pl.BlockSpec(memory_space=pltpu.VMEM)] * len(outs),
        compiler_params=pltpu.CompilerParams(vmem_limit_bytes=limit << 20),
        cost_estimate=pl.CostEstimate(flops=flops, bytes_accessed=moved, transcendentals=0),
    )(*args)


def shaped(shape, dtype):
    return jax.ShapeDtypeStruct(shape, dtype)


def in_hbm(value):
    return pltpu.with_memory_space_constraint(value, pltpu.HBM)


def lanes(head):
    return pl.ds(pl.multiple_of(head * DH, DH), DH)


def member(group, k):
    return lax.bitwise_xor(lax.rem(lax.axis_index("ctx"), group), k)


def place(k, n):
    out = 0
    bit = 1
    while bit < n:
        out = out * 2 + (k // bit) % 2
        bit *= 2
    return out


def start_all(copies):
    for copy in copies:
        copy.start()
    return copies


def wait_all(copies):
    for copy in copies:
        copy.wait()


def columns(group, k, width):
    return pl.ds(pl.multiple_of(member(group, k) * width, width), width)


def states_of(group, share, ks, key_ref, value_ref, state_refs):
    for ref, k in zip(state_refs, ks):
        for i in range(share):
            h = lanes(member(group, k) * share + i)
            ref[i] = dot(key_ref[:, h], value_ref[:, h], 0, 0).astype(BF16)


def first_kernel(group, share, ks, key_hbm, value_hbm, cotangent_hbm, *refs):
    *state_refs, key_ref, value_ref, part_ref, sems = refs
    part = cotangent_hbm.at[:, pl.ds(0, part_ref.shape[1])]
    pairs = ((key_hbm, key_ref), (value_hbm, value_ref), (part, part_ref))
    copies = start_all(
        [pltpu.make_async_copy(src, dst, sems.at[n]) for n, (src, dst) in enumerate(pairs)]
    )
    wait_all(copies[:2])
    states_of(group, share, ks, key_ref, value_ref, state_refs)
    wait_all(copies[2:])


def second_kernel(group, share, ks, key_ref, value_ref, query_hbm, cotangent_hbm, *refs):
    *state_refs, query_ref, part_ref, sems = refs
    width = part_ref.shape[1]
    part = cotangent_hbm.at[:, pl.ds(cotangent_hbm.shape[1] - width, width)]
    pairs = ((query_hbm, query_ref), (part, part_ref))
    copies = start_all(
        [pltpu.make_async_copy(src, dst, sems.at[n]) for n, (src, dst) in enumerate(pairs)]
    )
    states_of(group, share, ks, key_ref, value_ref, state_refs)
    wait_all(copies)


def loading_states(kernel, group, share, ks, held, fresh, cotangent):
    rows, model = cotangent.shape
    vmem, hbm = (pl.BlockSpec(memory_space=space) for space in (pltpu.VMEM, pltpu.HBM))
    tokens = fresh[0].shape[0]
    outs = [shaped((share, DH, DH), BF16)] * len(ks) + [shaped(a.shape, a.dtype) for a in fresh]
    outs.append(shaped((rows, model // BACK_CHUNKS), BF16))
    return pl.pallas_call(
        functools.partial(kernel, group, share, ks),
        name="state",
        out_shape=outs,
        in_specs=[vmem] * len(held) + [hbm] * (len(fresh) + 1),
        out_specs=[vmem] * len(outs),
        scratch_shapes=[pltpu.SemaphoreType.DMA((len(fresh) + 1,))],
        compiler_params=pltpu.CompilerParams(vmem_limit_bytes=4 << 20),
        cost_estimate=pl.CostEstimate(
            flops=2 * tokens * DH * DH * share * len(ks), bytes_accessed=1 << 20, transcendentals=0
        ),
    )(*held, *map(in_hbm, fresh), in_hbm(cotangent))


def causal_mask(n):
    row = lax.broadcasted_iota(jnp.int32, (n, n), 0)
    col = lax.broadcasted_iota(jnp.int32, (n, n), 1)
    return col <= row


def load_copies(start, weight_hbm, weight_ref, sems):
    rows = weight_ref.shape[0] // LOADS
    width = weight_ref.shape[1]
    return [
        pltpu.make_async_copy(
            weight_hbm.at[pl.ds(n * rows, rows), pl.ds(start, width)],
            weight_ref.at[pl.ds(n * rows, rows)],
            sems.at[n],
        )
        for n in range(LOADS)
    ]


def loading_call(kernel, outs, args, weight, start, stop, flops):
    features = weight.shape[0]
    vmem = pl.BlockSpec(memory_space=pltpu.VMEM)
    *outs, weight = pl.pallas_call(
        functools.partial(kernel, start),
        out_shape=outs + [pltpu.VMEM((features, stop - start), BF16)],
        in_specs=[vmem] * len(args) + [pl.BlockSpec(memory_space=pltpu.HBM)],
        out_specs=[vmem] * (len(outs) + 1),
        scratch_shapes=[pltpu.SemaphoreType.DMA((LOADS,))],
        compiler_params=pltpu.CompilerParams(vmem_limit_bytes=8 << 20),
        cost_estimate=pl.CostEstimate(
            flops=flops, bytes_accessed=2 * features * (stop - start), transcendentals=0
        ),
    )(*args, in_hbm(weight))
    return outs, weight


def after_starts(copies, compute):
    if copies:
        pl.when(lax.axis_index("ctx") >= 0)(compute)
    else:
        compute()
    wait_all(copies)


def inner_kernel(group, share, sides, load, query_ref, key_ref, value_ref, *refs):
    weight_hbm, *outs, weight_ref, sems = refs
    inners, intras = outs[:2], outs[2:]
    copies = start_all(load_copies(load, weight_hbm, weight_ref, sems))

    def compute():
        mask = causal_mask(query_ref.shape[0])
        for side, ks in enumerate(sides):
            for h, cols, n, i in member_heads(group, share, ks):
                scores = dot(query_ref[:, cols], key_ref[:, cols], 1, 1)
                inner = jnp.where(mask, scores, 0.0).astype(BF16)
                inners[side][n * share + i] = inner
                intras[side][:, h] = dot(inner, value_ref[:, cols], 1, 0)

    after_starts(copies, compute)


def member_heads(group, share, ks):
    for n, k in enumerate(ks):
        for i in range(share):
            here = slice((n * share + i) * DH, (n * share + i + 1) * DH)
            yield here, lanes(member(group, k) * share + i), n, i


def row_starts(n_head, rows):
    me = lax.axis_index("head")
    return [
        pl.multiple_of(place(lax.bitwise_xor(me, j), n_head) * rows, rows) for j in range(n_head)
    ]


def norm_kernel(group, share, ks, n_head, query_ref, intra_ref, gain_ref, *refs):
    state_refs, (attn_ref, normed_ref) = refs[: len(ks)], refs[len(ks) :]
    rows = query_ref.shape[0] // n_head
    starts = row_starts(n_head, rows)
    for h, cols, n, i in member_heads(group, share, ks):
        attn = intra_ref[:, h] + dot(query_ref[:, cols], state_refs[n][i], 1, 0)
        attn_ref[:, h] = attn
        scale = lax.rsqrt(jnp.mean(attn * attn, axis=-1, keepdims=True) + EPS)
        normed = (attn * scale * gain_ref[:, cols]).astype(BF16)
        for j, start in enumerate(starts):
            normed_ref[pl.ds(start, rows), h] = normed[j * rows : (j + 1) * rows]


def grad_kernel(group, share, ks, n_head, query_ref, attn_ref, back_ref, gain_ref, grad_ref, *state_refs):
    rows = query_ref.shape[0] // n_head
    starts = row_starts(n_head, rows)
    for h, cols, n, i in member_heads(group, share, ks):
        attn = attn_ref[:, h]
        back = jnp.concatenate([back_ref[pl.ds(start, rows), cols] for start in starts], axis=0)
        back = back * gain_ref[:, cols]
        scale = lax.rsqrt(jnp.mean(attn * attn, axis=-1, keepdims=True) + EPS)
        lean = jnp.mean(back * attn, axis=-1, keepdims=True)
        grad = (scale * (back - attn * (scale * scale * lean))).astype(BF16)
        grad_ref[:, h] = grad
        state_refs[n][i] = dot(query_ref[:, cols], grad, 0, 0).astype(BF16)


def local_kernel(group, share, ks, query_ref, key_ref, value_ref, *refs):
    inners, grads, state_refs = refs[:2], refs[2:4], refs[4:-3]
    query_grad_ref, key_part_ref, value_part_ref = refs[-3:]
    mask = causal_mask(query_ref.shape[0])
    for h, cols, n, i in member_heads(group, share, ks):
        side, at = min(ks[n], 1), max(ks[n] - 1, 0) * share + i
        grad = grads[side][:, at * DH : (at + 1) * DH]
        inner_grad = jnp.where(mask, dot(grad, value_ref[:, cols], 1, 1), 0.0).astype(BF16)
        query_grad_ref[:, h] = (
            dot(inner_grad, key_ref[:, cols], 1, 0) + dot(grad, state_refs[n][i], 1, 1)
        ).astype(BF16)
        key_part_ref[:, h] = dot(inner_grad, query_ref[:, cols], 0, 0)
        value_part_ref[:, h] = dot(inners[side][at], grad, 0, 0)


def part_columns(k, width):
    return (0, k * width) if k < EARLY else (1, (k - EARLY) * width)


def finish_heads(group, share, ks, refs, key_grad_ref, value_grad_ref):
    key_ref, value_ref, *refs = refs
    key_parts, value_parts, state_refs = refs[:2], refs[2:4], refs[4:]
    for h, cols, n, i in member_heads(group, share, ks):
        state = state_refs[n][i]
        call_number, at = part_columns(ks[n], share * DH)
        here = slice(at + i * DH, at + (i + 1) * DH)
        key_grad = key_parts[call_number][:, here] + dot(value_ref[:, cols], state, 1, 1)
        key_grad_ref[:, h] = key_grad.astype(BF16)
        value_grad = value_parts[call_number][:, here] + dot(key_ref[:, cols], state, 1, 0)
        value_grad_ref[:, h] = value_grad.astype(BF16)
        yield h, cols, n * share + i


def finish_chunk(keep_ref, received_ref, out_ref):
    out_ref[...] = (keep_ref[...] + received_ref[...].astype(F32)).astype(BF16)


def own_final_kernel(group, share, ks, count, *refs):
    refs, (keep_ref, received_ref, *query_refs), outs, held, sems = (
        refs[:count], refs[count : count + 4], refs[count + 4 : -4], refs[-4:-1], refs[-1],
    )
    layer_out, query_grad, key_grad, value_grad = outs
    key_grad_ref, value_grad_ref, out_ref = held
    width = share * DH
    copies = []

    def send(source, target):
        copies.extend(start_all([pltpu.make_async_copy(source, target, sems.at[len(copies)])]))

    for k in range(group):
        call_number, at = part_columns(k, width)
        send(query_refs[call_number].at[:, pl.ds(at, width)], query_grad.at[:, columns(group, k, width)])
    finish_chunk(keep_ref, received_ref, out_ref)
    send(out_ref, layer_out.at[:, pl.ds(0, out_ref.shape[1])])
    for h, cols, _ in finish_heads(group, share, ks, refs, key_grad_ref, value_grad_ref):
        send(key_grad_ref.at[:, h], key_grad.at[:, cols])
        send(value_grad_ref.at[:, h], value_grad.at[:, cols])
    wait_all(copies)


def last_kernel(group, share, ks, count, *refs):
    refs, (keep_ref, received_ref), outs, held, sems = (
        refs[:count], refs[count : count + 2], refs[-7:-4], refs[-4:-1], refs[-1],
    )
    layer_out, key_grad, value_grad = outs
    key_grad_ref, value_grad_ref, out_ref = held
    copies = []

    def send(source, target):
        copies.extend(start_all([pltpu.make_async_copy(source, target, sems.at[len(copies)])]))

    for h, cols, _ in finish_heads(group, share, ks, refs, key_grad_ref, value_grad_ref):
        send(key_grad_ref.at[:, h], key_grad.at[:, cols])
        send(value_grad_ref.at[:, h], value_grad.at[:, cols])
    finish_chunk(keep_ref, received_ref, out_ref)
    split = layer_out.shape[1] - out_ref.shape[1]
    send(out_ref, layer_out.at[:, pl.ds(split, out_ref.shape[1])])
    wait_all(copies)


def final_part(kernel, group, share, ks, args, chunk, extra, before, outs):
    tokens = args[0].shape[0]
    vmem, hbm = (pl.BlockSpec(memory_space=space) for space in (pltpu.VMEM, pltpu.HBM))
    operands = [*args, *chunk, *extra]
    buffer = pltpu.VMEM((tokens, len(ks) * share * DH), BF16)
    copies = group + 1 + 2 * share * len(ks)
    return pl.pallas_call(
        functools.partial(kernel, group, share, ks, len(args)),
        out_shape=outs,
        in_specs=[vmem] * len(operands) + [hbm] * len(before),
        out_specs=[hbm] * len(outs),
        input_output_aliases={len(operands) + n: n for n in range(len(before))},
        scratch_shapes=[
            buffer, buffer, pltpu.VMEM(chunk[0].shape, BF16), pltpu.SemaphoreType.DMA((copies,))
        ],
        compiler_params=pltpu.CompilerParams(vmem_limit_bytes=4 << 20),
        cost_estimate=pl.CostEstimate(
            flops=4 * tokens * DH * DH * share * len(ks), bytes_accessed=3 << 20, transcendentals=0
        ),
    )(*operands, *before)


def back_kernel(count, load, near_ref, far_ref, *refs):
    weight_refs, refs = refs[:count], refs[count:]
    if load is not None:
        before_refs, (weight_hbm, out_ref, next_ref, sems) = refs[:-4], refs[-4:]
        copies = start_all(load_copies(load, weight_hbm, next_ref, sems))
    else:
        before_refs, out_ref, copies = refs[:-1], refs[-1], []

    def compute():
        full = jnp.concatenate([near_ref[...], far_ref[...]], axis=0)
        step = 256
        for i in range(out_ref.shape[1] // step):
            cols = slice(i * step, (i + 1) * step)
            out, at = None, 0
            for ref in weight_refs:
                depth = ref.shape[1]
                term = dot(full[:, at : at + depth], ref[cols], 1, 1)
                out = term if out is None else out + term
                at += depth
            for ref in before_refs:
                out = out + ref[:, cols]
            out_ref[:, cols] = out

    after_starts(copies, compute)


def pack_kernel(first_ref, second_ref, out_ref):
    rows = first_ref.shape[0]
    out_ref[:rows] = first_ref[...]
    out_ref[rows:] = second_ref[...]


def forward_kernel(group, count, load, own_ref, other_ref, *refs):
    weight_refs, refs = refs[:count], refs[count:]
    copies = []
    if load is not None:
        weight_hbm, *refs, next_ref, sems = refs
        copies = start_all(load_copies(load, weight_hbm, next_ref, sems))
    keep_ref, send_ref = refs
    half = keep_ref.shape[0]
    depth = own_ref.shape[1]
    step = 512

    def compute():
        at = 0
        for weight_ref in weight_refs:
            for first in range(0, weight_ref.shape[1], step):
                cols, source = slice(at, at + step), slice(first, first + step)
                out = dot(own_ref[...], weight_ref[columns(group, 0, depth), source], 1, 0)
                for k in range(1, group):
                    here = slice((k - 1) * depth, k * depth)
                    out = out + dot(
                        other_ref[:, here], weight_ref[columns(group, k, depth), source], 1, 0
                    )
                keep_ref[:, cols] = out[:half]
                send_ref[:, cols] = out[half:].astype(BF16)
                at += step

    after_starts(copies, compute)


def swap(value, axis, size, bit):
    return lax.ppermute(value, axis, [(i, i ^ bit) for i in range(size)])


def total_kernel(*refs):
    total = refs[0][...].astype(F32)
    for ref in refs[1:-1]:
        total = total + ref[...].astype(F32)
    refs[-1][...] = total.astype(BF16)


def split_kernel(group, forward, *refs):
    received, partners, outs = refs[:group], refs[group:-group], refs[-group:]
    position = lax.axis_index("ctx")
    before = jnp.zeros(outs[0].shape, F32)
    for n, ref in enumerate(partners):
        high = lax.rem(lax.div(position, group << n), 2)
        before = before + (high if forward else 1 - high).astype(F32) * ref[...].astype(F32)
    terms = [ref[...].astype(F32) for ref in received]
    for k, out in enumerate(outs):
        total = before
        for j, term in enumerate(terms):
            if j != k:
                mine, its = member(group, k), member(group, j)
                counts = its < mine if forward else its > mine
                total = total + jnp.where(counts, 1.0, 0.0) * term
        out[...] = total.astype(BF16)


def exclusive_scan(states, group, n_ctx, forward):
    like = shaped(states[0].shape, BF16)
    received = [states[0]]
    received += [swap(states[k], "ctx", n_ctx, k) for k in range(1, group)]
    bit = group
    while bit < n_ctx:
        (total,) = call(total_kernel, [like], received, 0, 4)
        received.append(swap(total, "ctx", n_ctx, bit))
        bit *= 2
    own, *others = call(
        functools.partial(split_kernel, group, forward), [like] * group, received, 0, 4
    )
    return [own] + [swap(o, "ctx", n_ctx, k + 1) for k, o in enumerate(others)]


def fold_kernel(keep_ref, received_ref, kept_ref, send_ref):
    rows = kept_ref.shape[0]
    kept_ref[...] = keep_ref[:rows] + received_ref[:rows].astype(F32)
    send_ref[...] = (keep_ref[rows:] + received_ref[rows:].astype(F32)).astype(BF16)


def gather(part, n_head):
    bit = n_head // 2
    other = swap(part, "head", n_head, bit)
    while bit > 1:
        bit //= 2
        both = shaped((2 * part.shape[0], part.shape[1]), BF16)
        (part,) = call(pack_kernel, [both], [part, other], 0, 2)
        other = swap(part, "head", n_head, bit)
    return [part, other]


def per_device(n_ctx, n_head, queries, key_rows, value_rows, norm_gain, out_weight, out_cotangent):
    return layer(n_ctx, n_head, queries, key_rows, value_rows, norm_gain, out_weight, out_cotangent)


def layer(n_ctx, n_head, queries, key_rows, value_rows, norm_gain, out_weight, out_cotangent):
    tokens, width = queries.shape
    heads = width // DH
    group = min(GROUP, n_ctx)
    share = heads // group
    model = out_weight.shape[1]
    gain = norm_gain.reshape(1, width)
    part = shaped((share, DH, DH), BF16)
    sides = ((0,), tuple(range(1, group)))
    sizes = [share * DH * len(ks) for ks in sides]
    unit = 2 * tokens * DH * width
    order = [place(k, n_head) for k in range(n_head)]

    *sent, key_rows, value_rows, first = loading_states(
        first_kernel, group, share, sides[1], (), (key_rows, value_rows), out_cotangent
    )
    kept, queries, second = loading_states(
        second_kernel, group, share, sides[0], (key_rows, value_rows), (queries,), out_cotangent
    )
    pieces = [gather(p, n_head) for p in (first, second)]
    states = exclusive_scan([kept] + sent, group, n_ctx, True)
    squares = [shaped((share * len(ks), tokens, tokens), BF16) for ks in sides]
    blocks_f32 = [shaped((tokens, size), F32) for size in sizes]
    blocks_bf16 = [shaped((tokens, size), BF16) for size in sizes]
    middle = model // BACK_CHUNKS
    cut = (middle + model) // 2
    kernel = functools.partial(inner_kernel, group, share, sides)
    args = [queries, key_rows, value_rows]
    outs, first_weight = loading_call(
        kernel, squares + blocks_f32, args, out_weight, 0, middle, 4 * unit
    )
    inners, intras = outs[:2], outs[2:]
    back_shape = [shaped((tokens, width), F32)]
    flops = 2 * tokens * width * middle
    kernel = functools.partial(back_kernel, 1)
    (back,), second_weight = loading_call(
        kernel, back_shape, pieces[0] + [first_weight], out_weight, middle, cut, flops
    )

    attns, normeds = [], []
    for n, ks in enumerate(sides):
        attn, normed = call(
            functools.partial(norm_kernel, group, share, ks, n_head),
            [blocks_f32[n], blocks_bf16[n]],
            [queries, intras[n], gain] + [states[k] for k in ks],
            unit // 2,
        )
        attns.append(attn)
        normeds.append(normed)
    products = [shaped((tokens // 2, middle), t) for t in (F32, BF16)]
    kernel = functools.partial(forward_kernel, group, 1)
    first_product, third_weight = loading_call(
        kernel, products, normeds + [first_weight], out_weight, cut, model, flops
    )
    late_weights = [second_weight, third_weight]
    kernel = functools.partial(back_kernel, 2, None)
    (back,) = call(kernel, back_shape, pieces[1] + late_weights + [back], flops)
    kernel = functools.partial(forward_kernel, group, 2, None)
    second_product = call(kernel, products, normeds + late_weights, flops)
    grads, grad_states = [], []
    for n, ks in enumerate(sides):
        grad, *state = call(
            functools.partial(grad_kernel, group, share, ks, n_head),
            [blocks_bf16[n]] + [part] * len(ks),
            [queries, attns[n], back, gain],
            unit // 2,
        )
        grads.append(grad)
        grad_states += state
    later_states = exclusive_scan(grad_states, group, n_ctx, False)

    chunks = []
    for kept, sent in (first_product, second_product):
        span = kept.shape[1]
        arrived = swap(sent, "head", n_head, 1)
        bit = 2
        while bit < n_head:
            rows = kept.shape[0] // 2
            kept, sent = call(
                fold_kernel,
                [shaped((rows, span), F32), shaped((rows, span), BF16)],
                [kept, arrived],
                0,
                4,
            )
            arrived = swap(sent, "head", n_head, bit)
            bit *= 2
        chunks.append((kept, arrived))

    query_grads, parts = [], []
    halves = (tuple(range(EARLY)), tuple(range(EARLY, group)))
    for ks in halves:
        shape = (tokens, share * DH * len(ks))
        query_grad, *part = call(
            functools.partial(local_kernel, group, share, ks),
            [shaped(shape, BF16), shaped(shape, F32), shaped(shape, F32)],
            [queries, key_rows, value_rows, *inners, *grads] + [states[k] for k in ks],
            4 * unit,
        )
        query_grads.append(query_grad)
        parts.append(part)
    parts = [part for pair in zip(*parts) for part in pair]
    args = [[key_rows, value_rows, *parts] + [later_states[k] for k in ks] for ks in sides]
    rows = [shaped((tokens, width), BF16)] * 3
    outs = [shaped((chunks[0][0].shape[0], model), BF16)] + rows
    layer_out, query_grad, *grads = final_part(
        own_final_kernel, group, share, sides[0], args[0], chunks[0], query_grads, [], outs
    )
    before = [layer_out, *grads]
    layer_out, key_grad, value_grad = final_part(
        last_kernel, group, share, sides[1], args[1], chunks[1], [], before, outs[:-1]
    )
    return layer_out, query_grad, key_grad, value_grad


def solution(mesh):
    in_specs = (
        P("ctx", "head"),
        P("ctx", "head"),
        P("ctx", "head"),
        P("head"),
        P("head", None),
        P(("ctx", "head"), None),
    )
    out_specs = (P(("ctx", "head"), None), P("ctx", "head"), P("ctx", "head"), P("ctx", "head"))
    body = functools.partial(per_device, mesh.shape["ctx"], mesh.shape["head"])
    return jax.shard_map(body, mesh=mesh, in_specs=in_specs, out_specs=out_specs, check_vma=False)
```

```python
import functools

import jax
import jax.numpy as jnp
from jax import lax
from jax.experimental import pallas as pl
from jax.experimental.pallas import tpu as pltpu
from jax.sharding import PartitionSpec as P


DH = 128
EPS = 1e-06
GROUP = 4
EARLY = 2
BACK_CHUNKS = 2
LOADS = 4
F32 = jnp.float32
BF16 = jnp.bfloat16


def dot(a, b, ca, cb):
    return lax.dot_general(a, b, (((ca,), (cb,)), ((), ())), preferred_element_type=F32)


def call(kernel, outs, args, flops, limit=8):
    moved = sum(a.size * a.dtype.itemsize for a in args) + sum(
        o.size * o.dtype.itemsize for o in outs
    )
    return pl.pallas_call(
        kernel,
        out_shape=outs,
        in_specs=[pl.BlockSpec(memory_space=pltpu.VMEM)] * len(args),
        out_specs=[pl.BlockSpec(memory_space=pltpu.VMEM)] * len(outs),
        compiler_params=pltpu.CompilerParams(vmem_limit_bytes=limit << 20),
        cost_estimate=pl.CostEstimate(flops=flops, bytes_accessed=moved, transcendentals=0),
    )(*args)


def shaped(shape, dtype):
    return jax.ShapeDtypeStruct(shape, dtype)


def in_hbm(value):
    return pltpu.with_memory_space_constraint(value, pltpu.HBM)


def lanes(head):
    return pl.ds(pl.multiple_of(head * DH, DH), DH)


def member(group, k):
    return lax.bitwise_xor(lax.rem(lax.axis_index("ctx"), group), k)


def place(k, n):
    out = 0
    bit = 1
    while bit < n:
        out = out * 2 + (k // bit) % 2
        bit *= 2
    return out


def start_all(copies):
    for copy in copies:
        copy.start()
    return copies


def wait_all(copies):
    for copy in copies:
        copy.wait()


def columns(group, k, width):
    return pl.ds(pl.multiple_of(member(group, k) * width, width), width)


def states_of(group, share, ks, key_ref, value_ref, state_refs):
    for ref, k in zip(state_refs, ks):
        for i in range(share):
            h = lanes(member(group, k) * share + i)
            ref[i] = dot(key_ref[:, h], value_ref[:, h], 0, 0).astype(BF16)


def first_kernel(group, share, ks, key_hbm, value_hbm, cotangent_hbm, *refs):
    *state_refs, key_ref, value_ref, part_ref, sems = refs
    part = cotangent_hbm.at[:, pl.ds(0, part_ref.shape[1])]
    pairs = ((key_hbm, key_ref), (value_hbm, value_ref), (part, part_ref))
    copies = start_all(
        [pltpu.make_async_copy(src, dst, sems.at[n]) for n, (src, dst) in enumerate(pairs)]
    )
    wait_all(copies[:2])
    states_of(group, share, ks, key_ref, value_ref, state_refs)
    wait_all(copies[2:])


def second_kernel(group, share, ks, key_ref, value_ref, query_hbm, cotangent_hbm, *refs):
    *state_refs, query_ref, part_ref, sems = refs
    width = part_ref.shape[1]
    part = cotangent_hbm.at[:, pl.ds(cotangent_hbm.shape[1] - width, width)]
    pairs = ((query_hbm, query_ref), (part, part_ref))
    copies = start_all(
        [pltpu.make_async_copy(src, dst, sems.at[n]) for n, (src, dst) in enumerate(pairs)]
    )
    states_of(group, share, ks, key_ref, value_ref, state_refs)
    wait_all(copies)


def loading_states(kernel, group, share, ks, held, fresh, cotangent):
    rows, model = cotangent.shape
    vmem, hbm = (pl.BlockSpec(memory_space=space) for space in (pltpu.VMEM, pltpu.HBM))
    tokens = fresh[0].shape[0]
    outs = [shaped((share, DH, DH), BF16)] * len(ks) + [shaped(a.shape, a.dtype) for a in fresh]
    outs.append(shaped((rows, model // BACK_CHUNKS), BF16))
    return pl.pallas_call(
        functools.partial(kernel, group, share, ks),
        name="state",
        out_shape=outs,
        in_specs=[vmem] * len(held) + [hbm] * (len(fresh) + 1),
        out_specs=[vmem] * len(outs),
        scratch_shapes=[pltpu.SemaphoreType.DMA((len(fresh) + 1,))],
        compiler_params=pltpu.CompilerParams(vmem_limit_bytes=4 << 20),
        cost_estimate=pl.CostEstimate(
            flops=2 * tokens * DH * DH * share * len(ks), bytes_accessed=1 << 20, transcendentals=0
        ),
    )(*held, *map(in_hbm, fresh), in_hbm(cotangent))


def causal_mask(n):
    row = lax.broadcasted_iota(jnp.int32, (n, n), 0)
    col = lax.broadcasted_iota(jnp.int32, (n, n), 1)
    return col <= row


def load_copies(start, weight_hbm, weight_ref, sems):
    rows = weight_ref.shape[0] // LOADS
    width = weight_ref.shape[1]
    return [
        pltpu.make_async_copy(
            weight_hbm.at[pl.ds(n * rows, rows), pl.ds(start, width)],
            weight_ref.at[pl.ds(n * rows, rows)],
            sems.at[n],
        )
        for n in range(LOADS)
    ]


def loading_call(kernel, outs, args, weight, start, stop, flops):
    features = weight.shape[0]
    vmem = pl.BlockSpec(memory_space=pltpu.VMEM)
    *outs, weight = pl.pallas_call(
        functools.partial(kernel, start),
        out_shape=outs + [pltpu.VMEM((features, stop - start), BF16)],
        in_specs=[vmem] * len(args) + [pl.BlockSpec(memory_space=pltpu.HBM)],
        out_specs=[vmem] * (len(outs) + 1),
        scratch_shapes=[pltpu.SemaphoreType.DMA((LOADS,))],
        compiler_params=pltpu.CompilerParams(vmem_limit_bytes=8 << 20),
        cost_estimate=pl.CostEstimate(
            flops=flops, bytes_accessed=2 * features * (stop - start), transcendentals=0
        ),
    )(*args, in_hbm(weight))
    return outs, weight


def after_starts(copies, compute):
    if copies:
        pl.when(lax.axis_index("ctx") >= 0)(compute)
    else:
        compute()
    wait_all(copies)


def inner_kernel(group, share, sides, load, query_ref, key_ref, value_ref, *refs):
    weight_hbm, *outs, weight_ref, sems = refs
    inners, intras = outs[:2], outs[2:]
    copies = start_all(load_copies(load, weight_hbm, weight_ref, sems))

    def compute():
        mask = causal_mask(query_ref.shape[0])
        for side, ks in enumerate(sides):
            for h, cols, n, i in member_heads(group, share, ks):
                scores = dot(query_ref[:, cols], key_ref[:, cols], 1, 1)
                inner = jnp.where(mask, scores, 0.0).astype(BF16)
                inners[side][n * share + i] = inner
                intras[side][:, h] = dot(inner, value_ref[:, cols], 1, 0)

    after_starts(copies, compute)


def member_heads(group, share, ks):
    for n, k in enumerate(ks):
        for i in range(share):
            here = slice((n * share + i) * DH, (n * share + i + 1) * DH)
            yield here, lanes(member(group, k) * share + i), n, i


def row_starts(n_head, rows):
    me = lax.axis_index("head")
    return [
        pl.multiple_of(place(lax.bitwise_xor(me, j), n_head) * rows, rows) for j in range(n_head)
    ]


def norm_kernel(group, share, ks, n_head, query_ref, intra_ref, gain_ref, *refs):
    state_refs, (attn_ref, normed_ref) = refs[: len(ks)], refs[len(ks) :]
    rows = query_ref.shape[0] // n_head
    starts = row_starts(n_head, rows)
    for h, cols, n, i in member_heads(group, share, ks):
        attn = intra_ref[:, h] + dot(query_ref[:, cols], state_refs[n][i], 1, 0)
        attn_ref[:, h] = attn
        scale = lax.rsqrt(jnp.mean(attn * attn, axis=-1, keepdims=True) + EPS)
        normed = (attn * scale * gain_ref[:, cols]).astype(BF16)
        for j, start in enumerate(starts):
            normed_ref[pl.ds(start, rows), h] = normed[j * rows : (j + 1) * rows]


def grad_kernel(group, share, ks, n_head, query_ref, attn_ref, back_ref, gain_ref, grad_ref, *state_refs):
    rows = query_ref.shape[0] // n_head
    starts = row_starts(n_head, rows)
    for h, cols, n, i in member_heads(group, share, ks):
        attn = attn_ref[:, h]
        back = jnp.concatenate([back_ref[pl.ds(start, rows), cols] for start in starts], axis=0)
        back = back * gain_ref[:, cols]
        scale = lax.rsqrt(jnp.mean(attn * attn, axis=-1, keepdims=True) + EPS)
        lean = jnp.mean(back * attn, axis=-1, keepdims=True)
        grad = (scale * (back - attn * (scale * scale * lean))).astype(BF16)
        grad_ref[:, h] = grad
        state_refs[n][i] = dot(query_ref[:, cols], grad, 0, 0).astype(BF16)


def local_kernel(group, share, ks, query_ref, key_ref, value_ref, *refs):
    inners, grads, state_refs = refs[:2], refs[2:4], refs[4:-3]
    query_grad_ref, key_part_ref, value_part_ref = refs[-3:]
    mask = causal_mask(query_ref.shape[0])
    for h, cols, n, i in member_heads(group, share, ks):
        side, at = min(ks[n], 1), max(ks[n] - 1, 0) * share + i
        grad = grads[side][:, at * DH : (at + 1) * DH]
        inner_grad = jnp.where(mask, dot(grad, value_ref[:, cols], 1, 1), 0.0).astype(BF16)
        query_grad_ref[:, h] = (
            dot(inner_grad, key_ref[:, cols], 1, 0) + dot(grad, state_refs[n][i], 1, 1)
        ).astype(BF16)
        key_part_ref[:, h] = dot(inner_grad, query_ref[:, cols], 0, 0)
        value_part_ref[:, h] = dot(inners[side][at], grad, 0, 0)


def part_columns(k, width):
    return (0, k * width) if k < EARLY else (1, (k - EARLY) * width)


def finish_heads(group, share, ks, refs, key_grad_ref, value_grad_ref):
    key_ref, value_ref, *refs = refs
    key_parts, value_parts, state_refs = refs[:2], refs[2:4], refs[4:]
    for h, cols, n, i in member_heads(group, share, ks):
        state = state_refs[n][i]
        call_number, at = part_columns(ks[n], share * DH)
        here = slice(at + i * DH, at + (i + 1) * DH)
        key_grad = key_parts[call_number][:, here] + dot(value_ref[:, cols], state, 1, 1)
        key_grad_ref[:, h] = key_grad.astype(BF16)
        value_grad = value_parts[call_number][:, here] + dot(key_ref[:, cols], state, 1, 0)
        value_grad_ref[:, h] = value_grad.astype(BF16)
        yield h, cols, n * share + i


def finish_chunk(keep_ref, received_ref, out_ref):
    out_ref[...] = (keep_ref[...] + received_ref[...].astype(F32)).astype(BF16)


def own_final_kernel(group, share, ks, count, *refs):
    refs, (keep_ref, received_ref, *query_refs), outs, held, sems = (
        refs[:count], refs[count : count + 4], refs[count + 4 : -4], refs[-4:-1], refs[-1],
    )
    layer_out, query_grad, key_grad, value_grad = outs
    key_grad_ref, value_grad_ref, out_ref = held
    width = share * DH
    copies = []

    def send(source, target):
        copies.extend(start_all([pltpu.make_async_copy(source, target, sems.at[len(copies)])]))

    for k in range(group):
        call_number, at = part_columns(k, width)
        send(query_refs[call_number].at[:, pl.ds(at, width)], query_grad.at[:, columns(group, k, width)])
    finish_chunk(keep_ref, received_ref, out_ref)
    send(out_ref, layer_out.at[:, pl.ds(0, out_ref.shape[1])])
    for h, cols, _ in finish_heads(group, share, ks, refs, key_grad_ref, value_grad_ref):
        send(key_grad_ref.at[:, h], key_grad.at[:, cols])
        send(value_grad_ref.at[:, h], value_grad.at[:, cols])
    wait_all(copies)


def last_kernel(group, share, ks, count, *refs):
    refs, (keep_ref, received_ref), outs, held, sems = (
        refs[:count], refs[count : count + 2], refs[-7:-4], refs[-4:-1], refs[-1],
    )
    layer_out, key_grad, value_grad = outs
    key_grad_ref, value_grad_ref, out_ref = held
    copies = []

    def send(source, target):
        copies.extend(start_all([pltpu.make_async_copy(source, target, sems.at[len(copies)])]))

    finish_chunk(keep_ref, received_ref, out_ref)
    split = layer_out.shape[1] - out_ref.shape[1]
    send(out_ref, layer_out.at[:, pl.ds(split, out_ref.shape[1])])
    for h, cols, _ in finish_heads(group, share, ks, refs, key_grad_ref, value_grad_ref):
        send(key_grad_ref.at[:, h], key_grad.at[:, cols])
        send(value_grad_ref.at[:, h], value_grad.at[:, cols])
    wait_all(copies)


def final_part(kernel, group, share, ks, args, chunk, extra, before, outs):
    tokens = args[0].shape[0]
    vmem, hbm = (pl.BlockSpec(memory_space=space) for space in (pltpu.VMEM, pltpu.HBM))
    operands = [*args, *chunk, *extra]
    buffer = pltpu.VMEM((tokens, len(ks) * share * DH), BF16)
    copies = group + 1 + 2 * share * len(ks)
    return pl.pallas_call(
        functools.partial(kernel, group, share, ks, len(args)),
        out_shape=outs,
        in_specs=[vmem] * len(operands) + [hbm] * len(before),
        out_specs=[hbm] * len(outs),
        input_output_aliases={len(operands) + n: n for n in range(len(before))},
        scratch_shapes=[
            buffer, buffer, pltpu.VMEM(chunk[0].shape, BF16), pltpu.SemaphoreType.DMA((copies,))
        ],
        compiler_params=pltpu.CompilerParams(vmem_limit_bytes=4 << 20),
        cost_estimate=pl.CostEstimate(
            flops=4 * tokens * DH * DH * share * len(ks), bytes_accessed=3 << 20, transcendentals=0
        ),
    )(*operands, *before)


def back_kernel(count, load, near_ref, far_ref, *refs):
    weight_refs, refs = refs[:count], refs[count:]
    if load is not None:
        before_refs, (weight_hbm, out_ref, next_ref, sems) = refs[:-4], refs[-4:]
        copies = start_all(load_copies(load, weight_hbm, next_ref, sems))
    else:
        before_refs, out_ref, copies = refs[:-1], refs[-1], []

    def compute():
        full = jnp.concatenate([near_ref[...], far_ref[...]], axis=0)
        step = 256
        for i in range(out_ref.shape[1] // step):
            cols = slice(i * step, (i + 1) * step)
            out, at = None, 0
            for ref in weight_refs:
                depth = ref.shape[1]
                term = dot(full[:, at : at + depth], ref[cols], 1, 1)
                out = term if out is None else out + term
                at += depth
            for ref in before_refs:
                out = out + ref[:, cols]
            out_ref[:, cols] = out

    after_starts(copies, compute)


def pack_kernel(first_ref, second_ref, out_ref):
    rows = first_ref.shape[0]
    out_ref[:rows] = first_ref[...]
    out_ref[rows:] = second_ref[...]


def forward_kernel(group, count, load, own_ref, other_ref, *refs):
    weight_refs, refs = refs[:count], refs[count:]
    copies = []
    if load is not None:
        weight_hbm, *refs, next_ref, sems = refs
        copies = start_all(load_copies(load, weight_hbm, next_ref, sems))
    keep_ref, send_ref = refs
    half = keep_ref.shape[0]
    depth = own_ref.shape[1]
    step = 512

    def compute():
        at = 0
        for weight_ref in weight_refs:
            for first in range(0, weight_ref.shape[1], step):
                cols, source = slice(at, at + step), slice(first, first + step)
                out = dot(own_ref[...], weight_ref[columns(group, 0, depth), source], 1, 0)
                for k in range(1, group):
                    here = slice((k - 1) * depth, k * depth)
                    out = out + dot(
                        other_ref[:, here], weight_ref[columns(group, k, depth), source], 1, 0
                    )
                keep_ref[:, cols] = out[:half]
                send_ref[:, cols] = out[half:].astype(BF16)
                at += step

    after_starts(copies, compute)


def swap(value, axis, size, bit):
    return lax.ppermute(value, axis, [(i, i ^ bit) for i in range(size)])


def total_kernel(*refs):
    total = refs[0][...].astype(F32)
    for ref in refs[1:-1]:
        total = total + ref[...].astype(F32)
    refs[-1][...] = total.astype(BF16)


def split_kernel(group, forward, *refs):
    received, partners, outs = refs[:group], refs[group:-group], refs[-group:]
    position = lax.axis_index("ctx")
    before = jnp.zeros(outs[0].shape, F32)
    for n, ref in enumerate(partners):
        high = lax.rem(lax.div(position, group << n), 2)
        before = before + (high if forward else 1 - high).astype(F32) * ref[...].astype(F32)
    terms = [ref[...].astype(F32) for ref in received]
    for k, out in enumerate(outs):
        total = before
        for j, term in enumerate(terms):
            if j != k:
                mine, its = member(group, k), member(group, j)
                counts = its < mine if forward else its > mine
                total = total + jnp.where(counts, 1.0, 0.0) * term
        out[...] = total.astype(BF16)


def exclusive_scan(states, group, n_ctx, forward):
    like = shaped(states[0].shape, BF16)
    received = [states[0]]
    received += [swap(states[k], "ctx", n_ctx, k) for k in range(1, group)]
    bit = group
    while bit < n_ctx:
        (total,) = call(total_kernel, [like], received, 0, 4)
        received.append(swap(total, "ctx", n_ctx, bit))
        bit *= 2
    own, *others = call(
        functools.partial(split_kernel, group, forward), [like] * group, received, 0, 4
    )
    return [own] + [swap(o, "ctx", n_ctx, k + 1) for k, o in enumerate(others)]


def fold_kernel(keep_ref, received_ref, kept_ref, send_ref):
    rows = kept_ref.shape[0]
    kept_ref[...] = keep_ref[:rows] + received_ref[:rows].astype(F32)
    send_ref[...] = (keep_ref[rows:] + received_ref[rows:].astype(F32)).astype(BF16)


def gather(part, n_head):
    bit = n_head // 2
    other = swap(part, "head", n_head, bit)
    while bit > 1:
        bit //= 2
        both = shaped((2 * part.shape[0], part.shape[1]), BF16)
        (part,) = call(pack_kernel, [both], [part, other], 0, 2)
        other = swap(part, "head", n_head, bit)
    return [part, other]


def per_device(n_ctx, n_head, queries, key_rows, value_rows, norm_gain, out_weight, out_cotangent):
    return layer(n_ctx, n_head, queries, key_rows, value_rows, norm_gain, out_weight, out_cotangent)


def layer(n_ctx, n_head, queries, key_rows, value_rows, norm_gain, out_weight, out_cotangent):
    tokens, width = queries.shape
    heads = width // DH
    group = min(GROUP, n_ctx)
    share = heads // group
    model = out_weight.shape[1]
    gain = norm_gain.reshape(1, width)
    part = shaped((share, DH, DH), BF16)
    sides = ((0,), tuple(range(1, group)))
    sizes = [share * DH * len(ks) for ks in sides]
    unit = 2 * tokens * DH * width
    order = [place(k, n_head) for k in range(n_head)]

    *sent, key_rows, value_rows, first = loading_states(
        first_kernel, group, share, sides[1], (), (key_rows, value_rows), out_cotangent
    )
    kept, queries, second = loading_states(
        second_kernel, group, share, sides[0], (key_rows, value_rows), (queries,), out_cotangent
    )
    pieces = [gather(p, n_head) for p in (first, second)]
    states = exclusive_scan([kept] + sent, group, n_ctx, True)
    squares = [shaped((share * len(ks), tokens, tokens), BF16) for ks in sides]
    blocks_f32 = [shaped((tokens, size), F32) for size in sizes]
    blocks_bf16 = [shaped((tokens, size), BF16) for size in sizes]
    middle = model // BACK_CHUNKS
    cut = (middle + model) // 2
    kernel = functools.partial(inner_kernel, group, share, sides)
    args = [queries, key_rows, value_rows]
    outs, first_weight = loading_call(
        kernel, squares + blocks_f32, args, out_weight, 0, middle, 4 * unit
    )
    inners, intras = outs[:2], outs[2:]
    back_shape = [shaped((tokens, width), F32)]
    flops = 2 * tokens * width * middle
    kernel = functools.partial(back_kernel, 1)
    (back,), second_weight = loading_call(
        kernel, back_shape, pieces[0] + [first_weight], out_weight, middle, cut, flops
    )

    attns, normeds = [], []
    for n, ks in enumerate(sides):
        attn, normed = call(
            functools.partial(norm_kernel, group, share, ks, n_head),
            [blocks_f32[n], blocks_bf16[n]],
            [queries, intras[n], gain] + [states[k] for k in ks],
            unit // 2,
        )
        attns.append(attn)
        normeds.append(normed)
    products = [shaped((tokens // 2, middle), t) for t in (F32, BF16)]
    kernel = functools.partial(forward_kernel, group, 1)
    first_product, third_weight = loading_call(
        kernel, products, normeds + [first_weight], out_weight, cut, model, flops
    )
    late_weights = [second_weight, third_weight]
    kernel = functools.partial(back_kernel, 2, None)
    (back,) = call(kernel, back_shape, pieces[1] + late_weights + [back], flops)
    kernel = functools.partial(forward_kernel, group, 2, None)
    second_product = call(kernel, products, normeds + late_weights, flops)
    grads, grad_states = [], []
    for n, ks in enumerate(sides):
        grad, *state = call(
            functools.partial(grad_kernel, group, share, ks, n_head),
            [blocks_bf16[n]] + [part] * len(ks),
            [queries, attns[n], back, gain],
            unit // 2,
        )
        grads.append(grad)
        grad_states += state
    later_states = exclusive_scan(grad_states, group, n_ctx, False)

    chunks = []
    for kept, sent in (first_product, second_product):
        span = kept.shape[1]
        arrived = swap(sent, "head", n_head, 1)
        bit = 2
        while bit < n_head:
            rows = kept.shape[0] // 2
            kept, sent = call(
                fold_kernel,
                [shaped((rows, span), F32), shaped((rows, span), BF16)],
                [kept, arrived],
                0,
                4,
            )
            arrived = swap(sent, "head", n_head, bit)
            bit *= 2
        chunks.append((kept, arrived))

    query_grads, parts = [], []
    halves = (tuple(range(EARLY)), tuple(range(EARLY, group)))
    for ks in halves:
        shape = (tokens, share * DH * len(ks))
        query_grad, *part = call(
            functools.partial(local_kernel, group, share, ks),
            [shaped(shape, BF16), shaped(shape, F32), shaped(shape, F32)],
            [queries, key_rows, value_rows, *inners, *grads] + [states[k] for k in ks],
            4 * unit,
        )
        query_grads.append(query_grad)
        parts.append(part)
    parts = [part for pair in zip(*parts) for part in pair]
    ends = ((0, group - 1), tuple(range(1, group - 1)))
    args = [[key_rows, value_rows, *parts] + [later_states[k] for k in ks] for ks in ends]
    rows = [shaped((tokens, width), BF16)] * 3
    outs = [shaped((chunks[0][0].shape[0], model), BF16)] + rows
    layer_out, query_grad, *grads = final_part(
        own_final_kernel, group, share, ends[0], args[0], chunks[0], query_grads, [], outs
    )
    before = [layer_out, *grads]
    layer_out, key_grad, value_grad = final_part(
        last_kernel, group, share, ends[1], args[1], chunks[1], [], before, outs[:-1]
    )
    return layer_out, query_grad, key_grad, value_grad


def solution(mesh):
    in_specs = (
        P("ctx", "head"),
        P("ctx", "head"),
        P("ctx", "head"),
        P("head"),
        P("head", None),
        P(("ctx", "head"), None),
    )
    out_specs = (P(("ctx", "head"), None), P("ctx", "head"), P("ctx", "head"), P("ctx", "head"))
    body = functools.partial(per_device, mesh.shape["ctx"], mesh.shape["head"])
    return jax.shard_map(body, mesh=mesh, in_specs=in_specs, out_specs=out_specs, check_vma=False)
```

```python
import functools

import jax
import jax.numpy as jnp
from jax import lax
from jax.experimental import pallas as pl
from jax.experimental.pallas import tpu as pltpu
from jax.sharding import PartitionSpec as P


DH = 128
EPS = 1e-06
GROUP = 4
EARLY = 2
BACK_CHUNKS = 2
LOADS = 4
SPLIT = 2
F32 = jnp.float32
BF16 = jnp.bfloat16


def dot(a, b, ca, cb):
    return lax.dot_general(a, b, (((ca,), (cb,)), ((), ())), preferred_element_type=F32)


def call(kernel, outs, args, flops, limit=8):
    moved = sum(a.size * a.dtype.itemsize for a in args) + sum(
        o.size * o.dtype.itemsize for o in outs
    )
    return pl.pallas_call(
        kernel,
        out_shape=outs,
        in_specs=[pl.BlockSpec(memory_space=pltpu.VMEM)] * len(args),
        out_specs=[pl.BlockSpec(memory_space=pltpu.VMEM)] * len(outs),
        compiler_params=pltpu.CompilerParams(vmem_limit_bytes=limit << 20),
        cost_estimate=pl.CostEstimate(flops=flops, bytes_accessed=moved, transcendentals=0),
    )(*args)


def shaped(shape, dtype):
    return jax.ShapeDtypeStruct(shape, dtype)


def in_hbm(value):
    return pltpu.with_memory_space_constraint(value, pltpu.HBM)


def lanes(head):
    return pl.ds(pl.multiple_of(head * DH, DH), DH)


def member(group, k):
    return lax.bitwise_xor(lax.rem(lax.axis_index("ctx"), group), k)


def place(k, n):
    out = 0
    bit = 1
    while bit < n:
        out = out * 2 + (k // bit) % 2
        bit *= 2
    return out


def start_all(copies):
    for copy in copies:
        copy.start()
    return copies


def wait_all(copies):
    for copy in copies:
        copy.wait()


def columns(group, k, width):
    return pl.ds(pl.multiple_of(member(group, k) * width, width), width)


def states_of(group, share, ks, key_ref, value_ref, state_refs):
    for ref, k in zip(state_refs, ks):
        for i in range(share):
            h = lanes(member(group, k) * share + i)
            ref[i] = dot(key_ref[:, h], value_ref[:, h], 0, 0).astype(BF16)


def first_kernel(group, share, ks, key_hbm, value_hbm, cotangent_hbm, *refs):
    *state_refs, key_ref, value_ref, part_ref, sems = refs
    part = cotangent_hbm.at[:, pl.ds(0, part_ref.shape[1])]
    rows = key_ref.shape[0] // SPLIT
    pairs = []
    for n in range(SPLIT):
        here = pl.ds(n * rows, rows)
        pairs += [(key_hbm.at[here], key_ref.at[here]), (value_hbm.at[here], value_ref.at[here])]
    pairs.append((part, part_ref))
    copies = start_all(
        [pltpu.make_async_copy(src, dst, sems.at[n]) for n, (src, dst) in enumerate(pairs)]
    )
    wait_all(copies[:-1])
    states_of(group, share, ks, key_ref, value_ref, state_refs)
    wait_all(copies[-1:])


def second_kernel(group, share, ks, key_ref, value_ref, query_hbm, cotangent_hbm, *refs):
    *state_refs, query_ref, part_ref, sems = refs
    width = part_ref.shape[1]
    part = cotangent_hbm.at[:, pl.ds(cotangent_hbm.shape[1] - width, width)]
    pairs = ((query_hbm, query_ref), (part, part_ref))
    copies = start_all(
        [pltpu.make_async_copy(src, dst, sems.at[n]) for n, (src, dst) in enumerate(pairs)]
    )
    states_of(group, share, ks, key_ref, value_ref, state_refs)
    wait_all(copies)


def loading_states(kernel, group, share, ks, held, fresh, cotangent):
    rows, model = cotangent.shape
    vmem, hbm = (pl.BlockSpec(memory_space=space) for space in (pltpu.VMEM, pltpu.HBM))
    tokens = fresh[0].shape[0]
    outs = [shaped((share, DH, DH), BF16)] * len(ks) + [shaped(a.shape, a.dtype) for a in fresh]
    outs.append(shaped((rows, model // BACK_CHUNKS), BF16))
    return pl.pallas_call(
        functools.partial(kernel, group, share, ks),
        name="state",
        out_shape=outs,
        in_specs=[vmem] * len(held) + [hbm] * (len(fresh) + 1),
        out_specs=[vmem] * len(outs),
        scratch_shapes=[pltpu.SemaphoreType.DMA((len(fresh) * SPLIT + 1,))],
        compiler_params=pltpu.CompilerParams(vmem_limit_bytes=4 << 20),
        cost_estimate=pl.CostEstimate(
            flops=2 * tokens * DH * DH * share * len(ks), bytes_accessed=1 << 20, transcendentals=0
        ),
    )(*held, *map(in_hbm, fresh), in_hbm(cotangent))


def causal_mask(n):
    row = lax.broadcasted_iota(jnp.int32, (n, n), 0)
    col = lax.broadcasted_iota(jnp.int32, (n, n), 1)
    return col <= row


def load_copies(start, weight_hbm, weight_ref, sems):
    rows = weight_ref.shape[0] // LOADS
    width = weight_ref.shape[1]
    return [
        pltpu.make_async_copy(
            weight_hbm.at[pl.ds(n * rows, rows), pl.ds(start, width)],
            weight_ref.at[pl.ds(n * rows, rows)],
            sems.at[n],
        )
        for n in range(LOADS)
    ]


def loading_call(kernel, outs, args, weight, start, stop, flops):
    features = weight.shape[0]
    vmem = pl.BlockSpec(memory_space=pltpu.VMEM)
    *outs, weight = pl.pallas_call(
        functools.partial(kernel, start),
        out_shape=outs + [pltpu.VMEM((features, stop - start), BF16)],
        in_specs=[vmem] * len(args) + [pl.BlockSpec(memory_space=pltpu.HBM)],
        out_specs=[vmem] * (len(outs) + 1),
        scratch_shapes=[pltpu.SemaphoreType.DMA((LOADS,))],
        compiler_params=pltpu.CompilerParams(vmem_limit_bytes=8 << 20),
        cost_estimate=pl.CostEstimate(
            flops=flops, bytes_accessed=2 * features * (stop - start), transcendentals=0
        ),
    )(*args, in_hbm(weight))
    return outs, weight


def after_starts(copies, compute):
    if copies:
        pl.when(lax.axis_index("ctx") >= 0)(compute)
    else:
        compute()
    wait_all(copies)


def inner_kernel(group, share, sides, load, query_ref, key_ref, value_ref, *refs):
    weight_hbm, *outs, weight_ref, sems = refs
    inners, intras = outs[:2], outs[2:]
    copies = start_all(load_copies(load, weight_hbm, weight_ref, sems))

    def compute():
        mask = causal_mask(query_ref.shape[0])
        for side, ks in enumerate(sides):
            for h, cols, n, i in member_heads(group, share, ks):
                scores = dot(query_ref[:, cols], key_ref[:, cols], 1, 1)
                inner = jnp.where(mask, scores, 0.0).astype(BF16)
                inners[side][n * share + i] = inner
                intras[side][:, h] = dot(inner, value_ref[:, cols], 1, 0)

    after_starts(copies, compute)


def member_heads(group, share, ks):
    for n, k in enumerate(ks):
        for i in range(share):
            here = slice((n * share + i) * DH, (n * share + i + 1) * DH)
            yield here, lanes(member(group, k) * share + i), n, i


def row_starts(n_head, rows):
    me = lax.axis_index("head")
    return [
        pl.multiple_of(place(lax.bitwise_xor(me, j), n_head) * rows, rows) for j in range(n_head)
    ]


def norm_kernel(group, share, ks, n_head, query_ref, intra_ref, gain_ref, *refs):
    state_refs, (attn_ref, normed_ref) = refs[: len(ks)], refs[len(ks) :]
    rows = query_ref.shape[0] // n_head
    starts = row_starts(n_head, rows)
    for h, cols, n, i in member_heads(group, share, ks):
        attn = intra_ref[:, h] + dot(query_ref[:, cols], state_refs[n][i], 1, 0)
        attn_ref[:, h] = attn
        scale = lax.rsqrt(jnp.mean(attn * attn, axis=-1, keepdims=True) + EPS)
        normed = (attn * scale * gain_ref[:, cols]).astype(BF16)
        for j, start in enumerate(starts):
            normed_ref[pl.ds(start, rows), h] = normed[j * rows : (j + 1) * rows]


def grad_kernel(group, share, ks, n_head, query_ref, attn_ref, back_ref, gain_ref, grad_ref, *state_refs):
    rows = query_ref.shape[0] // n_head
    starts = row_starts(n_head, rows)
    for h, cols, n, i in member_heads(group, share, ks):
        attn = attn_ref[:, h]
        back = jnp.concatenate([back_ref[pl.ds(start, rows), cols] for start in starts], axis=0)
        back = back * gain_ref[:, cols]
        scale = lax.rsqrt(jnp.mean(attn * attn, axis=-1, keepdims=True) + EPS)
        lean = jnp.mean(back * attn, axis=-1, keepdims=True)
        grad = (scale * (back - attn * (scale * scale * lean))).astype(BF16)
        grad_ref[:, h] = grad
        state_refs[n][i] = dot(query_ref[:, cols], grad, 0, 0).astype(BF16)


def local_kernel(group, share, ks, query_ref, key_ref, value_ref, *refs):
    inners, grads, state_refs = refs[:2], refs[2:4], refs[4:-3]
    query_grad_ref, key_part_ref, value_part_ref = refs[-3:]
    mask = causal_mask(query_ref.shape[0])
    for h, cols, n, i in member_heads(group, share, ks):
        side, at = min(ks[n], 1), max(ks[n] - 1, 0) * share + i
        grad = grads[side][:, at * DH : (at + 1) * DH]
        inner_grad = jnp.where(mask, dot(grad, value_ref[:, cols], 1, 1), 0.0).astype(BF16)
        query_grad_ref[:, h] = (
            dot(inner_grad, key_ref[:, cols], 1, 0) + dot(grad, state_refs[n][i], 1, 1)
        ).astype(BF16)
        key_part_ref[:, h] = dot(inner_grad, query_ref[:, cols], 0, 0)
        value_part_ref[:, h] = dot(inners[side][at], grad, 0, 0)


def part_columns(k, width):
    return (0, k * width) if k < EARLY else (1, (k - EARLY) * width)


def finish_heads(group, share, ks, refs, key_grad_ref, value_grad_ref):
    key_ref, value_ref, *refs = refs
    key_parts, value_parts, state_refs = refs[:2], refs[2:4], refs[4:]
    for h, cols, n, i in member_heads(group, share, ks):
        state = state_refs[n][i]
        call_number, at = part_columns(ks[n], share * DH)
        here = slice(at + i * DH, at + (i + 1) * DH)
        key_grad = key_parts[call_number][:, here] + dot(value_ref[:, cols], state, 1, 1)
        key_grad_ref[:, h] = key_grad.astype(BF16)
        value_grad = value_parts[call_number][:, here] + dot(key_ref[:, cols], state, 1, 0)
        value_grad_ref[:, h] = value_grad.astype(BF16)
        yield h, cols, n * share + i


def finish_chunk(keep_ref, received_ref, out_ref):
    out_ref[...] = (keep_ref[...] + received_ref[...].astype(F32)).astype(BF16)


def own_final_kernel(group, share, ks, count, *refs):
    refs, (keep_ref, received_ref, *query_refs), outs, held, sems = (
        refs[:count], refs[count : count + 4], refs[count + 4 : -4], refs[-4:-1], refs[-1],
    )
    layer_out, query_grad, key_grad, value_grad = outs
    key_grad_ref, value_grad_ref, out_ref = held
    width = share * DH
    copies = []

    def send(source, target):
        copies.extend(start_all([pltpu.make_async_copy(source, target, sems.at[len(copies)])]))

    for k in range(group):
        call_number, at = part_columns(k, width)
        send(query_refs[call_number].at[:, pl.ds(at, width)], query_grad.at[:, columns(group, k, width)])
    finish_chunk(keep_ref, received_ref, out_ref)
    send(out_ref, layer_out.at[:, pl.ds(0, out_ref.shape[1])])
    for h, cols, _ in finish_heads(group, share, ks, refs, key_grad_ref, value_grad_ref):
        send(key_grad_ref.at[:, h], key_grad.at[:, cols])
        send(value_grad_ref.at[:, h], value_grad.at[:, cols])
    wait_all(copies)


def last_kernel(group, share, ks, count, *refs):
    refs, (keep_ref, received_ref), outs, held, sems = (
        refs[:count], refs[count : count + 2], refs[-7:-4], refs[-4:-1], refs[-1],
    )
    layer_out, key_grad, value_grad = outs
    key_grad_ref, value_grad_ref, out_ref = held
    copies = []

    def send(source, target):
        copies.extend(start_all([pltpu.make_async_copy(source, target, sems.at[len(copies)])]))

    finish_chunk(keep_ref, received_ref, out_ref)
    split = layer_out.shape[1] - out_ref.shape[1]
    send(out_ref, layer_out.at[:, pl.ds(split, out_ref.shape[1])])
    for h, cols, _ in finish_heads(group, share, ks, refs, key_grad_ref, value_grad_ref):
        send(key_grad_ref.at[:, h], key_grad.at[:, cols])
        send(value_grad_ref.at[:, h], value_grad.at[:, cols])
    wait_all(copies)


def final_part(kernel, group, share, ks, args, chunk, extra, before, outs):
    tokens = args[0].shape[0]
    vmem, hbm = (pl.BlockSpec(memory_space=space) for space in (pltpu.VMEM, pltpu.HBM))
    operands = [*args, *chunk, *extra]
    buffer = pltpu.VMEM((tokens, len(ks) * share * DH), BF16)
    copies = group + 1 + 2 * share * len(ks)
    return pl.pallas_call(
        functools.partial(kernel, group, share, ks, len(args)),
        out_shape=outs,
        in_specs=[vmem] * len(operands) + [hbm] * len(before),
        out_specs=[hbm] * len(outs),
        input_output_aliases={len(operands) + n: n for n in range(len(before))},
        scratch_shapes=[
            buffer, buffer, pltpu.VMEM(chunk[0].shape, BF16), pltpu.SemaphoreType.DMA((copies,))
        ],
        compiler_params=pltpu.CompilerParams(vmem_limit_bytes=4 << 20),
        cost_estimate=pl.CostEstimate(
            flops=4 * tokens * DH * DH * share * len(ks), bytes_accessed=3 << 20, transcendentals=0
        ),
    )(*operands, *before)


def back_kernel(count, load, near_ref, far_ref, *refs):
    weight_refs, refs = refs[:count], refs[count:]
    if load is not None:
        before_refs, (weight_hbm, out_ref, next_ref, sems) = refs[:-4], refs[-4:]
        copies = start_all(load_copies(load, weight_hbm, next_ref, sems))
    else:
        before_refs, out_ref, copies = refs[:-1], refs[-1], []

    def compute():
        full = jnp.concatenate([near_ref[...], far_ref[...]], axis=0)
        step = 256
        for i in range(out_ref.shape[1] // step):
            cols = slice(i * step, (i + 1) * step)
            out, at = None, 0
            for ref in weight_refs:
                depth = ref.shape[1]
                term = dot(full[:, at : at + depth], ref[cols], 1, 1)
                out = term if out is None else out + term
                at += depth
            for ref in before_refs:
                out = out + ref[:, cols]
            out_ref[:, cols] = out

    after_starts(copies, compute)


def pack_kernel(first_ref, second_ref, out_ref):
    rows = first_ref.shape[0]
    out_ref[:rows] = first_ref[...]
    out_ref[rows:] = second_ref[...]


def forward_kernel(group, count, load, own_ref, other_ref, *refs):
    weight_refs, refs = refs[:count], refs[count:]
    copies = []
    if load is not None:
        weight_hbm, *refs, next_ref, sems = refs
        copies = start_all(load_copies(load, weight_hbm, next_ref, sems))
    keep_ref, send_ref = refs
    half = keep_ref.shape[0]
    depth = own_ref.shape[1]
    step = 512

    def compute():
        at = 0
        for weight_ref in weight_refs:
            for first in range(0, weight_ref.shape[1], step):
                cols, source = slice(at, at + step), slice(first, first + step)
                out = dot(own_ref[...], weight_ref[columns(group, 0, depth), source], 1, 0)
                for k in range(1, group):
                    here = slice((k - 1) * depth, k * depth)
                    out = out + dot(
                        other_ref[:, here], weight_ref[columns(group, k, depth), source], 1, 0
                    )
                keep_ref[:, cols] = out[:half]
                send_ref[:, cols] = out[half:].astype(BF16)
                at += step

    after_starts(copies, compute)


def swap(value, axis, size, bit):
    return lax.ppermute(value, axis, [(i, i ^ bit) for i in range(size)])


def total_kernel(*refs):
    total = refs[0][...].astype(F32)
    for ref in refs[1:-1]:
        total = total + ref[...].astype(F32)
    refs[-1][...] = total.astype(BF16)


def split_kernel(group, forward, *refs):
    received, partners, outs = refs[:group], refs[group:-group], refs[-group:]
    position = lax.axis_index("ctx")
    before = jnp.zeros(outs[0].shape, F32)
    for n, ref in enumerate(partners):
        high = lax.rem(lax.div(position, group << n), 2)
        before = before + (high if forward else 1 - high).astype(F32) * ref[...].astype(F32)
    terms = [ref[...].astype(F32) for ref in received]
    for k, out in enumerate(outs):
        total = before
        for j, term in enumerate(terms):
            if j != k:
                mine, its = member(group, k), member(group, j)
                counts = its < mine if forward else its > mine
                total = total + jnp.where(counts, 1.0, 0.0) * term
        out[...] = total.astype(BF16)


def exclusive_scan(states, group, n_ctx, forward):
    like = shaped(states[0].shape, BF16)
    received = [states[0]]
    received += [swap(states[k], "ctx", n_ctx, k) for k in range(1, group)]
    bit = group
    while bit < n_ctx:
        (total,) = call(total_kernel, [like], received, 0, 4)
        received.append(swap(total, "ctx", n_ctx, bit))
        bit *= 2
    own, *others = call(
        functools.partial(split_kernel, group, forward), [like] * group, received, 0, 4
    )
    return [own] + [swap(o, "ctx", n_ctx, k + 1) for k, o in enumerate(others)]


def fold_kernel(keep_ref, received_ref, kept_ref, send_ref):
    rows = kept_ref.shape[0]
    kept_ref[...] = keep_ref[:rows] + received_ref[:rows].astype(F32)
    send_ref[...] = (keep_ref[rows:] + received_ref[rows:].astype(F32)).astype(BF16)


def gather(part, n_head):
    bit = n_head // 2
    other = swap(part, "head", n_head, bit)
    while bit > 1:
        bit //= 2
        both = shaped((2 * part.shape[0], part.shape[1]), BF16)
        (part,) = call(pack_kernel, [both], [part, other], 0, 2)
        other = swap(part, "head", n_head, bit)
    return [part, other]


def per_device(n_ctx, n_head, queries, key_rows, value_rows, norm_gain, out_weight, out_cotangent):
    return layer(n_ctx, n_head, queries, key_rows, value_rows, norm_gain, out_weight, out_cotangent)


def layer(n_ctx, n_head, queries, key_rows, value_rows, norm_gain, out_weight, out_cotangent):
    tokens, width = queries.shape
    heads = width // DH
    group = min(GROUP, n_ctx)
    share = heads // group
    model = out_weight.shape[1]
    gain = norm_gain.reshape(1, width)
    part = shaped((share, DH, DH), BF16)
    sides = ((0,), tuple(range(1, group)))
    sizes = [share * DH * len(ks) for ks in sides]
    unit = 2 * tokens * DH * width
    order = [place(k, n_head) for k in range(n_head)]

    *sent, key_rows, value_rows, first = loading_states(
        first_kernel, group, share, sides[1], (), (key_rows, value_rows), out_cotangent
    )
    kept, queries, second = loading_states(
        second_kernel, group, share, sides[0], (key_rows, value_rows), (queries,), out_cotangent
    )
    pieces = [gather(p, n_head) for p in (first, second)]
    states = exclusive_scan([kept] + sent, group, n_ctx, True)
    squares = [shaped((share * len(ks), tokens, tokens), BF16) for ks in sides]
    blocks_f32 = [shaped((tokens, size), F32) for size in sizes]
    blocks_bf16 = [shaped((tokens, size), BF16) for size in sizes]
    middle = model // BACK_CHUNKS
    cut = (middle + model) // 2
    kernel = functools.partial(inner_kernel, group, share, sides)
    args = [queries, key_rows, value_rows]
    outs, first_weight = loading_call(
        kernel, squares + blocks_f32, args, out_weight, 0, middle, 4 * unit
    )
    inners, intras = outs[:2], outs[2:]
    back_shape = [shaped((tokens, width), F32)]
    flops = 2 * tokens * width * middle
    kernel = functools.partial(back_kernel, 1)
    (back,), second_weight = loading_call(
        kernel, back_shape, pieces[0] + [first_weight], out_weight, middle, cut, flops
    )

    attns, normeds = [], []
    for n, ks in enumerate(sides):
        attn, normed = call(
            functools.partial(norm_kernel, group, share, ks, n_head),
            [blocks_f32[n], blocks_bf16[n]],
            [queries, intras[n], gain] + [states[k] for k in ks],
            unit // 2,
        )
        attns.append(attn)
        normeds.append(normed)
    products = [shaped((tokens // 2, middle), t) for t in (F32, BF16)]
    kernel = functools.partial(forward_kernel, group, 1)
    first_product, third_weight = loading_call(
        kernel, products, normeds + [first_weight], out_weight, cut, model, flops
    )
    late_weights = [second_weight, third_weight]
    kernel = functools.partial(back_kernel, 2, None)
    (back,) = call(kernel, back_shape, pieces[1] + late_weights + [back], flops)
    kernel = functools.partial(forward_kernel, group, 2, None)
    second_product = call(kernel, products, normeds + late_weights, flops)
    grads, grad_states = [], []
    for n, ks in enumerate(sides):
        grad, *state = call(
            functools.partial(grad_kernel, group, share, ks, n_head),
            [blocks_bf16[n]] + [part] * len(ks),
            [queries, attns[n], back, gain],
            unit // 2,
        )
        grads.append(grad)
        grad_states += state
    later_states = exclusive_scan(grad_states, group, n_ctx, False)

    chunks = []
    for kept, sent in (first_product, second_product):
        span = kept.shape[1]
        arrived = swap(sent, "head", n_head, 1)
        bit = 2
        while bit < n_head:
            rows = kept.shape[0] // 2
            kept, sent = call(
                fold_kernel,
                [shaped((rows, span), F32), shaped((rows, span), BF16)],
                [kept, arrived],
                0,
                4,
            )
            arrived = swap(sent, "head", n_head, bit)
            bit *= 2
        chunks.append((kept, arrived))

    query_grads, parts = [], []
    halves = (tuple(range(EARLY)), tuple(range(EARLY, group)))
    for ks in halves:
        shape = (tokens, share * DH * len(ks))
        query_grad, *part = call(
            functools.partial(local_kernel, group, share, ks),
            [shaped(shape, BF16), shaped(shape, F32), shaped(shape, F32)],
            [queries, key_rows, value_rows, *inners, *grads] + [states[k] for k in ks],
            4 * unit,
        )
        query_grads.append(query_grad)
        parts.append(part)
    parts = [part for pair in zip(*parts) for part in pair]
    ends = ((0, group - 1), tuple(range(1, group - 1)))
    args = [[key_rows, value_rows, *parts] + [later_states[k] for k in ks] for ks in ends]
    rows = [shaped((tokens, width), BF16)] * 3
    outs = [shaped((chunks[0][0].shape[0], model), BF16)] + rows
    layer_out, query_grad, *grads = final_part(
        own_final_kernel, group, share, ends[0], args[0], chunks[0], query_grads, [], outs
    )
    before = [layer_out, *grads]
    layer_out, key_grad, value_grad = final_part(
        last_kernel, group, share, ends[1], args[1], chunks[1], [], before, outs[:-1]
    )
    return layer_out, query_grad, key_grad, value_grad


def solution(mesh):
    in_specs = (
        P("ctx", "head"),
        P("ctx", "head"),
        P("ctx", "head"),
        P("head"),
        P("head", None),
        P(("ctx", "head"), None),
    )
    out_specs = (P(("ctx", "head"), None), P("ctx", "head"), P("ctx", "head"), P("ctx", "head"))
    body = functools.partial(per_device, mesh.shape["ctx"], mesh.shape["head"])
    return jax.shard_map(body, mesh=mesh, in_specs=in_specs, out_specs=out_specs, check_vma=False)
```
